32 devices in a mesh: dp: 8 (over y, x, core), tensor: 4 (over z).
Axes of the slice: x: 2, y: 2, z: 4, core: 2. Of those that a mesh axis runs over, the one named last changes fastest.
Arguments:
- inputs: bfloat16 [8192, 1024], P(('dp', 'tensor')), may hold values from -6 to 6
- segments: int32 [8, 1024], P('dp'), may hold values from 0 to 15, never falling along the last dimension, each value on 1 to 512 neighbouring positions
- cotangent: bfloat16 [8192, 1024], P(('dp', 'tensor')), may hold values from -6 to 6
- norm_in: float32 [1024], replicated, may hold values from 0.5 to 1.5
- w_in: bfloat16 [1024, 6144], P('dp', 'tensor'), may hold values from -0.1875 to 0.1875
- w_alpha_beta: bfloat16 [1024, 16], P('dp', 'tensor'), may hold values from -0.1875 to 0.1875
- conv_weight: float32 [4, 4096], replicated, may hold values from -3 to 3
- a_log: float32 [8], replicated, may hold values from -6.5 to -2.5
- dt_bias: float32 [8], replicated, may hold values from -1 to 1
- out_gain: float32 [256], replicated, may hold values from 0.5 to 1.5
- w_out: bfloat16 [2048, 1024], P('tensor', 'dp'), may hold values from -0.125 to 0.125
- norm_ffn: float32 [1024], replicated, may hold values from 0.5 to 1.5
- w_gate: bfloat16 [1024, 2816], P('dp', 'tensor'), may hold values from -0.1875 to 0.1875
- w_up: bfloat16 [1024, 2816], P('dp', 'tensor'), may hold values from -0.1875 to 0.1875
- w_down: bfloat16 [2816, 1024], P('tensor', 'dp'), may hold values from -0.109375 to 0.109375
Outputs:
- output: bfloat16 [8192, 1024], P(('dp', 'tensor'))
- d_inputs: float32 [8192, 1024], P(('dp', 'tensor'))
- grad_norm_in: float32 [1024], replicated
- grad_w_in: float32 [1024, 6144], P('dp', 'tensor')
- grad_w_alpha_beta: float32 [1024, 16], P('dp', 'tensor')
- grad_conv_weight: float32 [4, 4096], replicated
- grad_a_log: float32 [8], replicated
- grad_dt_bias: float32 [8], replicated
- grad_out_gain: float32 [256], replicated
- grad_w_out: float32 [2048, 1024], P('tensor', 'dp')
- grad_norm_ffn: float32 [1024], replicated
- grad_w_gate: float32 [1024, 2816], P('dp', 'tensor')
- grad_w_up: float32 [1024, 2816], P('dp', 'tensor')
- grad_w_down: float32 [2816, 1024], P('tensor', 'dp')
The draws below stay inside these ranges and needn't reach their ends.
Inputs may be any that keep to these rules, and one draw needn't show every extreme that they name: `segments`: within a sequence the numbers never fall, and each number covers at most 512 positions.
All inputs are finite; a program needn't handle non-finite values.
Results may differ from the reference program's by a relative error of at most 0.017.
Values may be sent and summed in bfloat16 or wider, within the bound.
No kernel may reach another device: no remote copies, remote signals or barrier semaphores. Data moves between devices by JAX's collectives and lax.ppermute only.
A program may use at most 256 MiB of HBM per device.

```python
import math
import jax
import jax.numpy as jnp
import numpy as np
from jax import lax

D = 1024
H = 8
DK = 128
DV = 256
FF = 2816
CONV = 4
SPAN = 64
DOCS = 16
LEN = 1024
SEQS = 8
TOKENS = 8192


def strengthened(entries, rng, source, target, parts, factor):
    owner, partner = [(jnp.arange(entries.shape[dim]) // (entries.shape[dim] // parts)).reshape([-1 if axis == dim else 1 for axis in range(entries.ndim)]) for dim in (source, target)]
    chosen = jax.random.permutation(rng, parts)[partner]
    strong = (owner == chosen) | (owner == (partner + parts // 2) % parts)
    return jnp.where(strong, factor * entries, entries)


def level_of(stream_key, shape, shards, least, high):
    level, own = 1.0, jax.random.fold_in(stream_key, 6)
    for dim, parts in shards:
        draws = jnp.exp(jax.random.uniform(jax.random.fold_in(own, dim), (parts,), jnp.float32, least / len(shards), high / len(shards)))
        level = level * jnp.repeat(draws, shape[dim] // parts).reshape([-1 if axis == dim else 1 for axis in range(len(shape))])
    return level


def profile(amount, total, most, lean):
    portions = [(1 << 20) // math.isqrt(rank ** lean) + 1 for rank in range(2, amount + 1)]
    surplus, holding = total - most - (amount - 1), [1] * (amount - 1)
    while surplus > 0:
        free = [i for i in range(amount - 1) if holding[i] < most]
        mass, remaining = sum([portions[i] for i in free]), surplus
        for i in free:
            extra = min(most - holding[i], max(1, remaining * portions[i] // mass), surplus)
            holding[i] = holding[i] + extra
            surplus = surplus - extra
    return np.array([most] + holding)


def ragged_sizes(stream_key, amount, total, limit, skew):
    if amount == 2:
        one = jax.random.randint(stream_key, (), max(1, total - limit), min(limit, total - 1) + 1)
        return jnp.stack([one, total - one])
    lengths = jnp.asarray(profile(amount, total, limit, skew), jnp.int32)
    couples = (amount - 1) // 2
    source_of, taker = lengths[1:1 + 2 * couples:2], lengths[2:2 + 2 * couples:2]
    slack = jnp.minimum(source_of - 1, limit - taker)
    moved = jax.random.randint(jax.random.fold_in(stream_key, 1), (couples,), 0, 1 << 20) % (slack + 1)
    lengths = lengths.at[1:1 + 2 * couples:2].set(source_of - moved).at[2:2 + 2 * couples:2].set(taker + moved)
    return lengths[jax.random.permutation(jax.random.fold_in(stream_key, 2), amount)]


def bell_draw(own_key, dims, spread, bound, shards=(), held_as=jnp.bfloat16):
    values = spread * jax.random.normal(own_key, dims, jnp.float32)
    if shards:
        values = values * level_of(own_key, dims, shards, -0.22, 0.18)
    return jnp.clip(values, -bound, bound).astype(held_as)


def bell_draw_with(stream_key, extent, spread, reach, pieces, heavy, kind=jnp.bfloat16):
    drawn = spread * jax.random.normal(stream_key, extent, jnp.float32)
    if pieces:
        drawn = drawn * level_of(stream_key, extent, pieces, -0.22, 0.18)
    return jnp.clip(strengthened(drawn, jax.random.fold_in(stream_key, 3), *heavy), -reach, reach).astype(kind)


def setup_inputs(seed: int = 0) -> dict:
    arg_keys = jax.random.split(jax.random.key(seed), 16)
    inputs = bell_draw_with(arg_keys[0], (TOKENS, D), 1.0, 6.0, ((0, 32),), (0, 1, 32, 2.75))
    segments = jax.vmap(lambda own: jnp.searchsorted(jnp.cumsum(ragged_sizes(own, DOCS, LEN, LEN // 2, 2)), jnp.arange(LEN), side="right"))(jax.random.split(arg_keys[1], SEQS)).reshape((SEQS, LEN)).astype(jnp.int32)
    cotangent = bell_draw_with(arg_keys[2], (TOKENS, D), 1.0, 6.0, ((0, 32),), (0, 1, 32, 2.75))
    norm_in = jnp.clip(1.0 + 0.1 * jax.random.normal(arg_keys[3], (D,), jnp.float32), 0.5, 1.5)
    w_in = bell_draw(arg_keys[4], (D, H * (2 * DK + 2 * DV)), D ** -0.5, 0.1875, ((0, 8), (1, 4)))
    w_alpha_beta = bell_draw(arg_keys[5], (D, 2 * H), D ** -0.5, 0.1875, ((0, 8), (1, 4)))
    conv_weight = bell_draw(arg_keys[6], (CONV, H * (2 * DK + DV)), CONV ** -0.5, 3.0, (), jnp.float32)
    a_log = jnp.clip(jax.random.uniform(arg_keys[7], (H,), jnp.float32, -6.5, -2.5), -6.5, -2.5)
    dt_bias = jnp.clip(jax.random.uniform(arg_keys[8], (H,), jnp.float32, -1.0, 1.0), -1.0, 1.0)
    out_gain = jnp.clip(1.0 + 0.1 * jax.random.normal(arg_keys[9], (DV,), jnp.float32), 0.5, 1.5)
    w_out = bell_draw(arg_keys[10], (H * DV, D), (H * DV) ** -0.5, 0.125, ((0, 4), (1, 8)))
    norm_ffn = jnp.clip(1.0 + 0.1 * jax.random.normal(arg_keys[11], (D,), jnp.float32), 0.5, 1.5)
    w_gate = bell_draw(arg_keys[12], (D, FF), D ** -0.5, 0.1875, ((0, 8), (1, 4)))
    w_up = bell_draw(arg_keys[13], (D, FF), D ** -0.5, 0.1875, ((0, 8), (1, 4)))
    w_down = bell_draw(arg_keys[14], (FF, D), FF ** -0.5, 0.109375, ((0, 4), (1, 8)))
    return {"inputs": inputs, "segments": segments, "cotangent": cotangent, "norm_in": norm_in, "w_in": w_in, "w_alpha_beta": w_alpha_beta, "conv_weight": conv_weight, "a_log": a_log, "dt_bias": dt_bias, "out_gain": out_gain, "w_out": w_out, "norm_ffn": norm_ffn, "w_gate": w_gate, "w_up": w_up, "w_down": w_down}


EXACT_PRECISION = lax.Precision.HIGHEST
EPSILON = 1e-06

@jax.custom_vjp
def low(v):
    return lax.optimization_barrier(v.astype(jnp.bfloat16)).astype(jnp.float32)

@jax.custom_vjp
def low_back(v):
    return v

def low_keep(v):
    return (low(v), None)

def low_pass(kept, grad):
    return (grad,)

def back_keep(v):
    return (v, None)

def back_low(kept, grad):
    return (low(grad),)
low.defvjp(low_keep, low_pass)
low_back.defvjp(back_keep, back_low)

def rms_rows(values, gain):
    return values * lax.rsqrt(lax.optimization_barrier(jnp.mean(values * values, axis=-1, keepdims=True)) + EPSILON) * gain

def short_conv(signal, kernel, doc_ids):
    length = signal.shape[0]
    running = signal * kernel[0]
    for offset in range(1, kernel.shape[0]):
        shifted = jnp.concatenate([jnp.zeros((offset, signal.shape[1]), jnp.float32), signal[:length - offset]], axis=0)
        shifted_ids = jnp.concatenate([jnp.full((offset,), -1, jnp.int32), doc_ids[:length - offset]])
        running = running + jnp.where((shifted_ids == doc_ids)[:, None], shifted * kernel[offset], 0.0)
    return running

def delta_spans(queries, keys_in, values, decays, beta_gate, doc_ids):
    length = queries.shape[0]
    head_count = queries.shape[1]
    block_count = length // SPAN
    places = jnp.arange(SPAN)
    strict = places[:, None] > places[None, :]
    within = places[:, None] >= places[None, :]
    identity = jnp.eye(SPAN, dtype=jnp.float32)

    def to_blocks(array):
        return array.reshape((block_count, SPAN) + array.shape[1:])

    def block_step(carried, block_in):
        recurrent_carry_state, last_doc = carried
        query_b, key_b, value_b, decay_b, beta_b, doc_b = block_in
        cum_decay = jnp.transpose(jnp.cumsum(decay_b, axis=0))
        log_gap = cum_decay[:, :, None] - cum_decay[:, None, :]
        same_doc = doc_b[:, None] == doc_b[None, :]
        strict_mask = (strict & same_doc)[None]
        within_mask = (within & same_doc)[None]
        fade_strict = jnp.where(strict_mask, jnp.exp(jnp.where(strict_mask, log_gap, 0.0)), 0.0)
        fade_within = jnp.where(within_mask, jnp.exp(jnp.where(within_mask, log_gap, 0.0)), 0.0)
        visible_extent = jnp.where((doc_b == last_doc)[None, :], jnp.exp(cum_decay), 0.0)
        key_per_head = jnp.transpose(key_b, (1, 0, 2))
        query_per_head = jnp.transpose(query_b, (1, 0, 2))
        value_h = jnp.transpose(value_b, (1, 0, 2))
        beta_h = jnp.transpose(beta_b)
        key_key = jnp.einsum('hik,hjk->hij', key_per_head, key_per_head, precision=EXACT_PRECISION)
        system = identity[None] + beta_h[:, :, None] * key_key * fade_strict
        solved_values = jax.scipy.linalg.solve_triangular(system, beta_h[:, :, None] * value_h, lower=True, unit_diagonal=True)
        solved_keys = jax.scipy.linalg.solve_triangular(system, (beta_h * visible_extent)[:, :, None] * key_per_head, lower=True, unit_diagonal=True)
        delta_update_rows = solved_values - jnp.einsum('sty,syo->sto', solved_keys, recurrent_carry_state, precision=EXACT_PRECISION)
        query_key = jnp.einsum('hik,hjk->hij', query_per_head, key_per_head, precision=EXACT_PRECISION) * fade_within
        computed_output = visible_extent[:, :, None] * jnp.einsum('sty,syo->sto', query_per_head, recurrent_carry_state, precision=EXACT_PRECISION)
        computed_output = computed_output + jnp.einsum('hij,hjv->hiv', query_key, delta_update_rows, precision=EXACT_PRECISION)
        trailing_decay = jnp.where((doc_b == doc_b[-1])[None, :], jnp.exp(cum_decay[:, -1:] - cum_decay), 0.0)
        keep_factor = jnp.where(doc_b[-1] == last_doc, jnp.exp(cum_decay[:, -1]), 0.0)
        updated_state = keep_factor[:, None, None] * recurrent_carry_state
        updated_state = updated_state + jnp.einsum('fgb,fgn->fbn', trailing_decay[:, :, None] * key_per_head, delta_update_rows, precision=EXACT_PRECISION)
        return ((updated_state, doc_b[-1]), jnp.transpose(computed_output, (1, 0, 2)))
    initial = (jnp.zeros((head_count, keys_in.shape[2], values.shape[2]), jnp.float32), jnp.array(-1, jnp.int32))
    blocks_in = (to_blocks(queries), to_blocks(keys_in), to_blocks(values), to_blocks(decays), to_blocks(beta_gate), to_blocks(doc_ids))
    final_state, block_outs = lax.scan(jax.checkpoint(block_step), initial, blocks_in)
    return block_outs.reshape(length, head_count, values.shape[2])

def mixer_local(projected, alpha_beta, kernel, a_log, dt_bias, out_gain, doc_ids):
    length = projected.shape[0]
    head_count = a_log.shape[0]
    per_head = projected.reshape(length, head_count, 2 * DK + 2 * DV)
    conv_in = per_head[:, :, :2 * DK + DV].reshape(length, head_count * (2 * DK + DV))
    gate_out = per_head[:, :, 2 * DK + DV:]
    conv_out = jax.nn.silu(short_conv(conv_in, kernel, doc_ids)).reshape(length, head_count, 2 * DK + DV)
    queries = conv_out[:, :, :DK]
    keys_in = conv_out[:, :, DK:2 * DK]
    values = conv_out[:, :, 2 * DK:]
    queries = queries * lax.rsqrt(lax.optimization_barrier(jnp.sum(queries * queries, axis=-1, keepdims=True)) + EPSILON) * DK ** (-0.5)
    keys_in = keys_in * lax.rsqrt(lax.optimization_barrier(jnp.sum(keys_in * keys_in, axis=-1, keepdims=True)) + EPSILON)
    pair_rows = alpha_beta.reshape(length, head_count, 2)
    decays = -jnp.exp(a_log) * jax.nn.softplus(pair_rows[:, :, 0] + dt_bias)
    beta_gate = jax.nn.sigmoid(pair_rows[:, :, 1])
    recurrent = delta_spans(queries, keys_in, values, decays, beta_gate, doc_ids)
    normed = rms_rows(recurrent, out_gain)
    return (normed * jax.nn.silu(gate_out)).reshape(length, head_count * DV)

def layer(inputs, norm_in, w_in, w_alpha_beta, conv_weight, a_log, dt_bias, out_gain, w_out, norm_ffn, w_gate, w_up, w_down, doc_ids):
    normed_in = low(rms_rows(inputs, norm_in))
    projected = low_back(jnp.einsum('bld,de->ble', normed_in, w_in, precision=EXACT_PRECISION))
    alpha_beta = low_back(jnp.einsum('bld,de->ble', normed_in, w_alpha_beta, precision=EXACT_PRECISION))

    def one_sequence(proj_seq, pair_seq, ids_seq):
        return mixer_local(proj_seq, pair_seq, conv_weight, a_log, dt_bias, out_gain, ids_seq)
    gated = jax.vmap(one_sequence)(projected, alpha_beta, doc_ids)
    mixed = low_back(jnp.einsum('ble,ed->bld', low(gated), w_out, precision=EXACT_PRECISION))
    resid = inputs + mixed
    normed_ffn = low(rms_rows(resid, norm_ffn))
    gate_pre = low_back(jnp.einsum('bld,df->blf', normed_ffn, w_gate, precision=EXACT_PRECISION))
    up_pre = low_back(jnp.einsum('bld,df->blf', normed_ffn, w_up, precision=EXACT_PRECISION))
    hidden = low(jax.nn.silu(gate_pre) * up_pre)
    return resid + low_back(jnp.einsum('blf,fd->bld', hidden, w_down, precision=EXACT_PRECISION))

def reference(inputs, segments, cotangent, norm_in, w_in, w_alpha_beta, conv_weight, a_log, dt_bias, out_gain, w_out, norm_ffn, w_gate, w_up, w_down):
    per_group = math.gcd(SEQS, max(1, 4096 // LEN))
    group_count = SEQS // per_group
    weights = tuple((weight.astype(jnp.float32) for weight in (norm_in, w_in, w_alpha_beta, conv_weight, a_log, dt_bias, out_gain, w_out, norm_ffn, w_gate, w_up, w_down)))
    seq_inputs = inputs.astype(jnp.float32).reshape(group_count, per_group, LEN, D)
    seq_cots = cotangent.astype(jnp.float32).reshape(group_count, per_group, LEN, D)
    seq_ids = segments.reshape(group_count, per_group, LEN)
    zero_grads = tuple((jnp.zeros_like(weight) for weight in weights))

    def group_step(totals, group_in):
        group_x, group_cot, group_ids = group_in

        def forward(x_value, *params):
            return layer(x_value, *params, group_ids)
        computed_output, pullback = jax.vjp(forward, group_x, *weights)
        grads = pullback(group_cot)
        summed = tuple((total + grad for total, grad in zip(totals, grads[1:])))
        return (summed, (computed_output, grads[0]))
    totals, (results, input_grads) = lax.scan(group_step, zero_grads, (seq_inputs, seq_cots, seq_ids))
    output = results.reshape(TOKENS, D).astype(jnp.bfloat16)
    d_inputs = input_grads.reshape(TOKENS, D)
    return (output, d_inputs, totals[0], totals[1], totals[2], totals[3], totals[4], totals[5], totals[6], totals[7], totals[8], totals[9], totals[10], totals[11])
```

```python
import functools
import jax
import jax.numpy as jnp
from jax import lax
from jax.experimental import pallas as pl
from jax.experimental.pallas import tpu as pltpu

from jax.sharding import PartitionSpec as P

DK = 128
DV = 256
CONVW = 2 * DK + DV
HEADW = 2 * DK + 2 * DV
CHUNK = 128
EPSILON = 1e-06
F32 = jnp.float32
BF16 = jnp.bfloat16
NN = (((1,), (0,)), ((), ()))
NT = (((1,), (1,)), ((), ()))
TN = (((0,), (0,)), ((), ()))


def split(value):
    high = value.astype(BF16)
    return high, (value - high.astype(F32)).astype(BF16)


def dot1(left, right, dims=NN):
    return lax.dot_general(
        left.astype(BF16), right.astype(BF16), dims, preferred_element_type=F32
    )


def dot3(left, right, dims=NN):
    lh, ll = left if isinstance(left, tuple) else split(left)
    rh, rl = right if isinstance(right, tuple) else split(right)
    d = functools.partial(lax.dot_general, dimension_numbers=dims, preferred_element_type=F32)
    return d(lh, rh) + (d(lh, rl) + d(ll, rh))


def sigmoid(x):
    return 1.0 / (1.0 + jnp.exp(-x))


def softplus(x):
    return jnp.maximum(x, 0.0) + jnp.log(1.0 + jnp.exp(-jnp.abs(x)))


def place(shape, axis):
    return lax.broadcasted_iota(jnp.int32, shape, axis)


def cumulate(value, backwards=False):
    length = value.shape[0]
    row = place(value.shape, 0)
    step = 1
    while step < length:
        if backwards:
            moved = pltpu.roll(value, length - step, 0)
            value = value + jnp.where(row < length - step, moved, 0.0)
        else:
            moved = pltpu.roll(value, step, 0)
            value = value + jnp.where(row >= step, moved, 0.0)
        step *= 2
    return value


def conv_parts(before, rows, doc_before, docs):
    length = rows.shape[0]
    tall = jnp.concatenate([before, rows], axis=0)
    tall_docs = jnp.concatenate([doc_before, docs], axis=0)
    parts = [rows]
    for offset in range(1, 4):
        same = tall_docs[8 - offset : 8 - offset + length, :1] == docs[:, :1]
        parts.append(jnp.where(same, tall[8 - offset : 8 - offset + length], 0.0))
    return parts


def head_decay(cum, lane, docs, doc_row, doc_carried):
    square = docs.shape
    g_col = jnp.broadcast_to(cum[:, lane : lane + 1], square)
    g_row = jnp.transpose(g_col)
    row, col = place(square, 0), place(square, 1)
    seen = (row >= col) & (docs == doc_row)
    fade = jnp.where(seen, jnp.exp(jnp.where(seen, g_col - g_row, 0.0)), 0.0)
    strict = jnp.where(row > col, fade, 0.0)
    reach = jnp.where(docs == doc_carried, jnp.exp(g_col), 0.0)
    g_last = g_col[-1:, :]
    doc_last = docs[-1:, :]
    trail = jnp.where(docs == doc_last, jnp.exp(g_last - g_col), 0.0)
    keep = jnp.where(doc_last == doc_carried, jnp.exp(g_last), 0.0)
    return fade, strict, reach, trail, keep


def unit_lower_inverse(lower):
    square = lower.shape
    row, col = place(square, 0), place(square, 1)
    apart = row ^ col
    inverse = jnp.where(row == col, 1.0, jnp.where(apart == 1, -lower, 0.0))
    level = 1
    while (1 << level) < square[0]:
        part = jnp.where((apart >> level) == 1, lower, 0.0)
        pair = split(inverse)
        inverse = inverse - dot3(pair, dot3(part, pair))
        level += 1
    return inverse


def activations(proj_ref, before_ref, conv_ref, docs, doc_before, head):
    base = head * HEADW
    rows = proj_ref[:, base : base + CONVW]
    before = before_ref[:, base : base + CONVW]
    taps = conv_ref[:, head * CONVW : (head + 1) * CONVW]
    parts = conv_parts(before, rows, doc_before, docs)
    pre = sum(parts[s] * taps[s : s + 1] for s in range(4))
    gate = sigmoid(pre)
    post = pre * gate
    q_raw, k_raw, value = post[:, :DK], post[:, DK : 2 * DK], post[:, 2 * DK :]
    q_scale = lax.rsqrt(jnp.sum(q_raw * q_raw, axis=-1, keepdims=True) + EPSILON)
    k_scale = lax.rsqrt(jnp.sum(k_raw * k_raw, axis=-1, keepdims=True) + EPSILON)
    query = q_raw * q_scale * DK ** (-0.5)
    key = k_raw * k_scale
    return parts, taps, pre, gate, q_raw, k_raw, q_scale, k_scale, query, key, value


def doc_context(doc_ref, doc_before_ref, chunk):
    docs = doc_ref[...]
    doc_before = jnp.where(chunk > 0, doc_before_ref[...], -1.0)
    return docs, jnp.transpose(docs), doc_before, doc_before[-1:, :]


def forward_kernel(
    heads, proj_ref, before_ref, doc_ref, doc_before_ref, conv_ref, vec_ref, gain_ref,
    gated_ref, recur_ref, inverse_ref, solved_ref, mix_ref, key_ref, tilde_ref, start_ref, state,
):
    chunk = pl.program_id(0)

    @pl.when(chunk == 0)
    def _():
        state[...] = jnp.zeros_like(state)

    docs, doc_row, doc_before, doc_carried = doc_context(doc_ref, doc_before_ref, chunk)
    pair = proj_ref[:, heads * HEADW :]
    decay = -vec_ref[0:1, :] * softplus(pair + vec_ref[1:2, :])
    write = sigmoid(pair)
    cum = cumulate(decay)
    eye = place(docs.shape, 0) == place(docs.shape, 1)
    for head in range(heads):
        acts = activations(proj_ref, before_ref, conv_ref, docs, doc_before, head)
        query, key, value = acts[8:]
        fade, strict, reach, trail, keep = head_decay(cum, 2 * head, docs, doc_row, doc_carried)
        beta = write[:, 2 * head + 1 : 2 * head + 2]
        key_pair = split(key)
        both = dot3(jnp.concatenate([key, query], axis=0), key_pair, NT)
        key_key = both[:CHUNK] * strict
        mix = both[CHUNK:] * fade
        inverse = unit_lower_inverse(beta * key_key)
        rhs = jnp.concatenate([beta * reach * key, beta * value], axis=1)
        solved = dot3(inverse, rhs)
        trailing = jnp.transpose(trail * key)
        outer = dot3(jnp.concatenate([trailing, mix], axis=0), solved)
        step = jnp.where(eye, keep, 0.0) - outer[:CHUNK, :DK]
        q_tilde = reach * query - outer[CHUNK:, :DK]
        tilde = jnp.concatenate([step, q_tilde], axis=0)
        start = state[head]
        moved = dot3(tilde, start)
        state[head] = moved[:CHUNK] + outer[:CHUNK, DK:]
        recurrent = moved[CHUNK:] + outer[CHUNK:, DK:]
        inverse_ref[0, head] = inverse
        solved_ref[0, head] = solved
        mix_ref[0, head] = mix
        key_ref[0, head] = key_key
        tilde_ref[0, head] = tilde
        start_ref[0, head] = start
        recur_ref[:, head * DV : (head + 1) * DV] = recurrent
        scale = lax.rsqrt(jnp.mean(recurrent * recurrent, axis=-1, keepdims=True) + EPSILON)
        z = proj_ref[:, head * HEADW + CONVW : (head + 1) * HEADW]
        gated = recurrent * scale * gain_ref[...] * (z * sigmoid(z))
        gated_ref[:, head * DV : (head + 1) * DV] = gated.astype(BF16)


def backward_kernel(
    heads, chunks, proj_ref, before_ref, doc_ref, doc_before_ref, doc_after_ref,
    conv_ref, vec_ref, gain_ref, recur_ref, inverse_ref, solved_ref, mix_ref, key_ref, tilde_ref,
    start_ref, grad_ref,
    d_proj_ref, d_conv_ref, d_vec_ref, d_gain_ref, d_state, d_after,
):
    step_index = pl.program_id(0)
    chunk = chunks - 1 - step_index

    @pl.when(step_index == 0)
    def _():
        d_state[...] = jnp.zeros_like(d_state)
        d_after[...] = jnp.zeros_like(d_after)
        d_conv_ref[...] = jnp.zeros_like(d_conv_ref)
        d_vec_ref[...] = jnp.zeros_like(d_vec_ref)
        d_gain_ref[...] = jnp.zeros_like(d_gain_ref)

    docs, doc_row, doc_before, doc_carried = doc_context(doc_ref, doc_before_ref, chunk)
    tall_docs = jnp.concatenate([docs, doc_after_ref[...]], axis=0)
    pair = proj_ref[:, heads * HEADW :]
    shifted = pair + vec_ref[1:2, :]
    decay = -vec_ref[0:1, :] * softplus(shifted)
    write = sigmoid(pair)
    cum = cumulate(decay)
    lanes = place(docs.shape, 1)
    last_row = place(docs.shape, 0) == CHUNK - 1
    d_cum = jnp.zeros_like(docs)
    d_write = jnp.zeros_like(docs)
    for head in range(heads):
        acts = activations(proj_ref, before_ref, conv_ref, docs, doc_before, head)
        parts, taps, pre, gate, q_raw, k_raw, q_scale, k_scale, query, key, value = acts
        fade, strict, reach, trail, keep = head_decay(cum, 2 * head, docs, doc_row, doc_carried)
        beta = write[:, 2 * head + 1 : 2 * head + 2]
        grad = grad_ref[:, head * DV : (head + 1) * DV].astype(F32)
        recurrent = recur_ref[:, head * DV : (head + 1) * DV]
        scale = lax.rsqrt(jnp.mean(recurrent * recurrent, axis=-1, keepdims=True) + EPSILON)
        z = proj_ref[:, head * HEADW + CONVW : (head + 1) * HEADW]
        z_gate = sigmoid(z)
        unit = recurrent * scale
        gain = gain_ref[...]
        d_normed = grad * (z * z_gate)
        d_z = grad * unit * gain * (z_gate * (1.0 + z * (1.0 - z_gate)))
        d_gain_ref[...] += jnp.sum(d_normed * unit, axis=0, keepdims=True)
        weighted = d_normed * gain
        d_out = scale * (weighted - unit * jnp.mean(weighted * unit, axis=-1, keepdims=True))
        inverse = inverse_ref[0, head]
        solved = solved_ref[0, head]
        mix = mix_ref[0, head]
        key_key = key_ref[0, head]
        tilde = tilde_ref[0, head]
        start = start_ref[0, head]
        d_next = d_state[head]
        flow = jnp.concatenate([d_next, d_out], axis=0)
        d_state[head] = dot3(tilde, flow, TN)
        start_pair = split(start)
        delta = solved[:, DK:] - dot3(solved[:, :DK], start_pair)
        trailing = trail * key
        d_delta = dot3(jnp.concatenate([trailing, jnp.transpose(mix)], axis=1), flow)
        d_rhs = dot3(inverse, d_delta, TN)
        grads = jnp.concatenate([d_out, d_rhs], axis=0)
        outer = dot3(grads, delta, NT)
        onto = dot3(grads, start_pair, NT)
        d_mix = outer[:CHUNK]
        d_lower = -outer[CHUNK:]
        from_next = dot3(delta, d_next, NT)
        mixed = d_mix * fade
        lowered = d_lower * strict * beta
        d_query = reach * onto[:CHUNK] + dot3(mixed, key)
        d_key = (
            dot3(jnp.transpose(mixed), query)
            + dot3(lowered + jnp.transpose(lowered), key)
            + trail * from_next
            - beta * reach * onto[CHUNK:]
        )
        d_value = beta * d_rhs
        crossed = d_lower * key_key
        net = d_mix * mix + beta * crossed
        reach_col = reach[:, :1]
        sum_query = jnp.sum(query * onto[:CHUNK], axis=-1, keepdims=True)
        sum_key = jnp.sum(key * onto[CHUNK:], axis=-1, keepdims=True)
        sum_trail = jnp.sum(trailing * from_next, axis=-1, keepdims=True)
        d_beta = (
            jnp.sum(crossed, axis=-1, keepdims=True)
            + jnp.sum(d_rhs * value, axis=-1, keepdims=True)
            - reach_col * sum_key
        )
        d_g = (
            jnp.sum(net - jnp.transpose(net), axis=-1, keepdims=True)
            + reach_col * sum_query
            - beta * reach_col * sum_key
            - sum_trail
        )
        kept = keep[:, :1] * jnp.sum(
            jnp.sum(start * d_next, axis=-1, keepdims=True), axis=0, keepdims=True
        )
        d_last = jnp.sum(sum_trail, axis=0, keepdims=True) + kept
        d_g = d_g + jnp.where(last_row[:, :1], d_last, 0.0)
        d_cum = jnp.where(lanes == 2 * head, d_g, d_cum)
        d_write = jnp.where(lanes == 2 * head + 1, d_beta, d_write)
        d_q_raw = (
            (d_query - q_raw * (q_scale * q_scale) * jnp.sum(d_query * q_raw, axis=-1, keepdims=True))
            * q_scale * DK ** (-0.5)
        )
        d_k_raw = (
            d_key - k_raw * (k_scale * k_scale) * jnp.sum(d_key * k_raw, axis=-1, keepdims=True)
        ) * k_scale
        d_post = jnp.concatenate([d_q_raw, d_k_raw, d_value], axis=1)
        d_pre = d_post * gate * (1.0 + pre * (1.0 - gate))
        columns = slice(head * CONVW, (head + 1) * CONVW)
        d_conv_ref[:, columns] += jnp.concatenate(
            [jnp.sum(d_pre * parts[s], axis=0, keepdims=True) for s in range(4)], axis=0
        )
        tall = jnp.concatenate([d_pre, d_after[:, columns]], axis=0)
        d_rows = d_pre * taps[0:1]
        for offset in range(1, 4):
            same = tall_docs[offset : offset + CHUNK, :1] == docs[:, :1]
            d_rows = d_rows + jnp.where(
                same, tall[offset : offset + CHUNK] * taps[offset : offset + 1], 0.0
            )
        d_after[:, columns] = d_pre[:8]
        d_proj_ref[:, head * HEADW : head * HEADW + CONVW] = d_rows.astype(BF16)
        d_proj_ref[:, head * HEADW + CONVW : (head + 1) * HEADW] = d_z.astype(BF16)
    d_decay = cumulate(d_cum, backwards=True)
    d_shifted = d_decay * -vec_ref[0:1, :] * sigmoid(shifted)
    d_written = d_write * write * (1.0 - write)
    used = lanes < 2 * heads
    even = (lanes & 1) == 0
    d_proj_ref[:, heads * HEADW :] = jnp.where(used, jnp.where(even, d_shifted, d_written), 0.0).astype(BF16)
    d_vec_ref[0:1, :] += jnp.sum(d_decay * decay, axis=0, keepdims=True)
    d_vec_ref[1:2, :] += jnp.sum(d_shifted, axis=0, keepdims=True)


def chunk_specs(heads, chunks, where):
    per8 = CHUNK // 8

    def rows(width):
        return pl.BlockSpec((CHUNK, width), lambda c: (where(c), 0))

    def before(width):
        return pl.BlockSpec((8, width), lambda c: (jnp.maximum(where(c) * per8 - 1, 0), 0))

    def after(width):
        return pl.BlockSpec(
            (8, width), lambda c: (jnp.minimum((where(c) + 1) * per8, chunks * per8 - 1), 0)
        )

    def whole(shape):
        return pl.BlockSpec(shape, lambda c: (0,) * len(shape))

    def saved(height, width):
        return pl.BlockSpec((1, heads, height, width), lambda c: (where(c), 0, 0, 0))

    return rows, before, after, whole, saved


def saved_shapes(heads, chunks):
    sizes = ((CHUNK, CHUNK), (CHUNK, DK + DV), (CHUNK, CHUNK), (CHUNK, CHUNK), (2 * CHUNK, DK), (DK, DV))
    return sizes


def mixer_forward(projected, docs, taps, vectors, gain, interpret=False):
    length, width = projected.shape
    heads = (width - CHUNK) // HEADW
    chunks = length // CHUNK
    rows, before, after, whole, saved = chunk_specs(heads, chunks, lambda c: c)
    sizes = saved_shapes(heads, chunks)
    return pl.pallas_call(
        functools.partial(forward_kernel, heads),
        grid=(chunks,),
        in_specs=[
            rows(width), before(width), rows(CHUNK), before(CHUNK),
            whole((4, heads * CONVW)), whole((8, CHUNK)), whole((1, DV)),
        ],
        out_specs=[rows(heads * DV), rows(heads * DV)] + [saved(*s) for s in sizes],
        out_shape=[
            jax.ShapeDtypeStruct((length, heads * DV), BF16),
            jax.ShapeDtypeStruct((length, heads * DV), F32),
        ]
        + [jax.ShapeDtypeStruct((chunks, heads) + s, F32) for s in sizes],
        scratch_shapes=[pltpu.VMEM((heads, DK, DV), F32)],
        name="mixer_forward",
        interpret=interpret,
    )(projected, projected, docs, docs, taps, vectors, gain)


def mixer_backward(projected, docs, taps, vectors, gain, kept, grad, interpret=False):
    length, width = projected.shape
    heads = (width - CHUNK) // HEADW
    chunks = length // CHUNK
    rows, before, after, whole, saved = chunk_specs(heads, chunks, lambda c: chunks - 1 - c)
    sizes = saved_shapes(heads, chunks)
    return pl.pallas_call(
        functools.partial(backward_kernel, heads, chunks),
        grid=(chunks,),
        in_specs=[
            rows(width), before(width), rows(CHUNK), before(CHUNK), after(CHUNK),
            whole((4, heads * CONVW)), whole((8, CHUNK)), whole((1, DV)), rows(heads * DV),
        ]
        + [saved(*s) for s in sizes]
        + [rows(heads * DV)],
        out_specs=[
            rows(width), whole((4, heads * CONVW)), whole((8, CHUNK)), whole((1, DV)),
        ],
        out_shape=[
            jax.ShapeDtypeStruct((length, width), BF16),
            jax.ShapeDtypeStruct((4, heads * CONVW), F32),
            jax.ShapeDtypeStruct((8, CHUNK), F32),
            jax.ShapeDtypeStruct((1, DV), F32),
        ],
        scratch_shapes=[pltpu.VMEM((heads, DK, DV), F32), pltpu.VMEM((8, heads * CONVW), F32)],
        name="mixer_backward",
        interpret=interpret,
    )(projected, projected, docs, docs, docs, taps, vectors, gain, *kept, grad)


def rms_rows(values, gain):
    return values * lax.rsqrt(jnp.mean(values * values, axis=-1, keepdims=True) + EPSILON) * gain


def rms_back(values, gain, grad_normed):
    scale = lax.rsqrt(jnp.mean(values * values, axis=-1, keepdims=True) + EPSILON)
    weighted = grad_normed * gain
    inner = jnp.mean(weighted * values, axis=-1, keepdims=True)
    grad_values = scale * weighted - values * scale * scale * scale * inner
    return (grad_values, jnp.sum(grad_normed * values * scale, axis=0))


def times_transposed(left, right):
    return lax.dot_general(left, right, NT, preferred_element_type=F32)


def transposed_times(left, right):
    return lax.dot_general(left, right, TN, preferred_element_type=F32)


def ffn_front(resid, norm_ffn, w_gate, w_up, w_down):
    normed = rms_rows(resid, norm_ffn).astype(jnp.bfloat16)
    seq_rows = lax.all_gather(normed, "tensor", axis=0, tiled=True)
    whole_gate, whole_up, whole_down = (
        lax.all_gather(w_gate, "dp", axis=0, tiled=True),
        lax.all_gather(w_up, "dp", axis=0, tiled=True),
        lax.all_gather(w_down, "dp", axis=1, tiled=True),
    )
    gate_pre = jnp.dot(seq_rows, whole_gate, preferred_element_type=jnp.float32)
    up_pre = jnp.dot(seq_rows, whole_up, preferred_element_type=jnp.float32)
    hidden = (jax.nn.silu(gate_pre) * up_pre).astype(jnp.bfloat16)
    return (seq_rows, whole_gate, whole_up, whole_down, gate_pre, up_pre, hidden)


def local(
    inputs,
    segments,
    cotangent,
    norm_in,
    w_in,
    w_alpha_beta,
    conv_weight,
    a_log,
    dt_bias,
    out_gain,
    w_out,
    norm_ffn,
    w_gate,
    w_up,
    w_down,
):
    doc_ids = segments[0]
    part_index = lax.axis_index("tensor")
    head_count = a_log.shape[0] // lax.axis_size("tensor")
    conv_width = head_count * (2 * DK + DV)
    conv_mine = lax.dynamic_slice_in_dim(conv_weight, part_index * conv_width, conv_width, 1)
    alog_mine = lax.dynamic_slice_in_dim(a_log, part_index * head_count, head_count, 0)
    bias_mine = lax.dynamic_slice_in_dim(dt_bias, part_index * head_count, head_count, 0)

    length = doc_ids.shape[0]
    docs = jnp.broadcast_to(doc_ids.astype(F32)[:, None], (length, CHUNK))
    vectors = jnp.zeros((8, CHUNK), F32)
    vectors = vectors.at[0, 0 : 2 * head_count : 2].set(jnp.exp(alog_mine))
    vectors = vectors.at[1, 0 : 2 * head_count : 2].set(bias_mine)
    gain_row = out_gain[None, :]

    input_rows = inputs.astype(jnp.float32)
    normed = rms_rows(input_rows, norm_in).astype(BF16)
    seq_rows = lax.all_gather(normed, "tensor", axis=0, tiled=True)
    joined = jnp.concatenate(
        [w_in, jnp.pad(w_alpha_beta, ((0, 0), (0, CHUNK - w_alpha_beta.shape[1])))], axis=1
    )
    whole_in = lax.all_gather(joined, "dp", axis=0, tiled=True)
    whole_out = lax.all_gather(w_out, "dp", axis=1, tiled=True)
    projected = jnp.dot(seq_rows, whole_in, preferred_element_type=F32)
    gated, *kept = mixer_forward(projected, docs, conv_mine, vectors, gain_row)
    resid = input_rows + lax.psum_scatter(
        jnp.dot(gated, whole_out, preferred_element_type=jnp.float32),
        "tensor",
        scatter_dimension=0,
        tiled=True,
    )
    ffn_seq, whole_gate, whole_up, whole_down, gate_pre, up_pre, hidden = ffn_front(
        resid, norm_ffn, w_gate, w_up, w_down
    )
    output = (
        resid
        + lax.psum_scatter(
            jnp.dot(hidden, whole_down, preferred_element_type=jnp.float32).astype(jnp.bfloat16),
            "tensor",
            scatter_dimension=0,
            tiled=True,
        ).astype(jnp.float32)
    ).astype(jnp.bfloat16)
    back_seq = lax.all_gather(cotangent, "tensor", axis=0, tiled=True)
    d_hidden = times_transposed(back_seq, whole_down)
    sigmoid_gate = jax.nn.sigmoid(gate_pre)
    d_up = (d_hidden * gate_pre * sigmoid_gate).astype(jnp.bfloat16)
    d_gate = (d_hidden * up_pre * sigmoid_gate * (1.0 + gate_pre * (1.0 - sigmoid_gate))).astype(
        jnp.bfloat16
    )
    d_normed_ffn = lax.psum_scatter(
        (times_transposed(d_gate, whole_gate) + times_transposed(d_up, whole_up)).astype(
            jnp.bfloat16
        ),
        "tensor",
        scatter_dimension=0,
        tiled=True,
    ).astype(jnp.float32)
    resid_from_norm, gain_ffn_part = rms_back(resid, norm_ffn, d_normed_ffn)
    d_resid = cotangent.astype(jnp.float32) + resid_from_norm
    mixer_back_seq = lax.all_gather(d_resid.astype(jnp.bfloat16), "tensor", axis=0, tiled=True)
    d_gated = times_transposed(mixer_back_seq, whole_out)
    d_projected, d_conv, d_vectors, d_gain_row = mixer_backward(
        projected, docs, conv_mine, vectors, gain_row, kept, d_gated
    )
    d_alog = d_vectors[0, 0 : 2 * head_count : 2]
    d_bias = d_vectors[1, 0 : 2 * head_count : 2]
    d_gain_out = d_gain_row[0]
    d_normed_in = lax.psum_scatter(
        times_transposed(d_projected, whole_in).astype(BF16),
        "tensor",
        scatter_dimension=0,
        tiled=True,
    ).astype(jnp.float32)
    input_from_norm, gain_in_part = rms_back(input_rows, norm_in, d_normed_in)
    d_inputs = d_resid + input_from_norm
    conv_full = lax.dynamic_update_slice_in_dim(
        jnp.zeros(conv_weight.shape, jnp.float32), d_conv, part_index * conv_width, 1
    )
    alog_full = lax.dynamic_update_slice_in_dim(
        jnp.zeros(a_log.shape, jnp.float32), d_alog, part_index * head_count, 0
    )
    bias_full = lax.dynamic_update_slice_in_dim(
        jnp.zeros(dt_bias.shape, jnp.float32), d_bias, part_index * head_count, 0
    )
    small_sums = lax.psum(
        (gain_in_part, gain_ffn_part, conv_full, alog_full, bias_full, d_gain_out), ("dp", "tensor")
    )
    owned_joined, owned_out, owned_gate, owned_up, owned_down = (
        lax.psum_scatter(
            transposed_times(seq_rows, d_projected), "dp", scatter_dimension=0, tiled=True
        ),
        lax.psum_scatter(
            transposed_times(mixer_back_seq, gated), "dp", scatter_dimension=0, tiled=True
        ),
        lax.psum_scatter(transposed_times(ffn_seq, d_gate), "dp", scatter_dimension=0, tiled=True),
        lax.psum_scatter(transposed_times(ffn_seq, d_up), "dp", scatter_dimension=0, tiled=True),
        lax.psum_scatter(transposed_times(back_seq, hidden), "dp", scatter_dimension=0, tiled=True),
    )
    return (
        output,
        d_inputs,
        small_sums[0],
        owned_joined[:, : w_in.shape[1]],
        owned_joined[:, w_in.shape[1] : w_in.shape[1] + w_alpha_beta.shape[1]],
        small_sums[2],
        small_sums[3],
        small_sums[4],
        small_sums[5],
        jnp.transpose(owned_out),
        small_sums[1],
        owned_gate,
        owned_up,
        jnp.transpose(owned_down),
    )


def solution(mesh):
    return jax.shard_map(
        local,
        mesh=mesh,
        in_specs=(
            P(("dp", "tensor"), None),
            P("dp", None),
            P(("dp", "tensor"), None),
            P(),
            P("dp", "tensor"),
            P("dp", "tensor"),
            P(),
            P(),
            P(),
            P(),
            P("tensor", "dp"),
            P(),
            P("dp", "tensor"),
            P("dp", "tensor"),
            P("tensor", "dp"),
        ),
        out_specs=(
            P(("dp", "tensor"), None),
            P(("dp", "tensor"), None),
            P(),
            P("dp", "tensor"),
            P("dp", "tensor"),
            P(),
            P(),
            P(),
            P(),
            P("tensor", "dp"),
            P(),
            P("dp", "tensor"),
            P("dp", "tensor"),
            P("tensor", "dp"),
        ),
        check_vma=False,
    )
```

```python
import functools
import jax
import jax.numpy as jnp
from jax import lax
from jax.experimental import pallas as pl
from jax.experimental.pallas import tpu as pltpu

from jax.sharding import PartitionSpec as P

DK = 128
DV = 256
CONVW = 2 * DK + DV
HEADW = 2 * DK + 2 * DV
CHUNK = 128
EPSILON = 1e-06
F32 = jnp.float32
BF16 = jnp.bfloat16
NN = (((1,), (0,)), ((), ()))
NT = (((1,), (1,)), ((), ()))
TN = (((0,), (0,)), ((), ()))


def split(value):
    high = value.astype(BF16)
    return high, (value - high.astype(F32)).astype(BF16)


def dot1(left, right, dims=NN):
    return lax.dot_general(
        left.astype(BF16), right.astype(BF16), dims, preferred_element_type=F32
    )


def dot3(left, right, dims=NN):
    lh, ll = left if isinstance(left, tuple) else split(left)
    rh, rl = right if isinstance(right, tuple) else split(right)
    d = functools.partial(lax.dot_general, dimension_numbers=dims, preferred_element_type=F32)
    return d(lh, rh) + (d(lh, rl) + d(ll, rh))


def sigmoid(x):
    return 1.0 / (1.0 + jnp.exp(-x))


def softplus(x):
    return jnp.maximum(x, 0.0) + jnp.log(1.0 + jnp.exp(-jnp.abs(x)))


def place(shape, axis):
    return lax.broadcasted_iota(jnp.int32, shape, axis)


def cumulate(value, backwards=False):
    length = value.shape[0]
    row = place(value.shape, 0)
    step = 1
    while step < length:
        if backwards:
            moved = pltpu.roll(value, length - step, 0)
            value = value + jnp.where(row < length - step, moved, 0.0)
        else:
            moved = pltpu.roll(value, step, 0)
            value = value + jnp.where(row >= step, moved, 0.0)
        step *= 2
    return value


def conv_parts(before, rows, doc_before, docs):
    length = rows.shape[0]
    tall = jnp.concatenate([before, rows], axis=0)
    tall_docs = jnp.concatenate([doc_before, docs], axis=0)
    parts = [rows]
    for offset in range(1, 4):
        same = tall_docs[8 - offset : 8 - offset + length, :1] == docs[:, :1]
        parts.append(jnp.where(same, tall[8 - offset : 8 - offset + length], 0.0))
    return parts


def head_decay(cum, lane, docs, doc_row, doc_carried):
    square = docs.shape
    g_col = jnp.broadcast_to(cum[:, lane : lane + 1], square)
    g_row = jnp.transpose(g_col)
    row, col = place(square, 0), place(square, 1)
    seen = (row >= col) & (docs == doc_row)
    fade = jnp.where(seen, jnp.exp(jnp.where(seen, g_col - g_row, 0.0)), 0.0)
    strict = jnp.where(row > col, fade, 0.0)
    reach = jnp.where(docs == doc_carried, jnp.exp(g_col), 0.0)
    g_last = g_col[-1:, :]
    doc_last = docs[-1:, :]
    trail = jnp.where(docs == doc_last, jnp.exp(g_last - g_col), 0.0)
    keep = jnp.where(doc_last == doc_carried, jnp.exp(g_last), 0.0)
    return fade, strict, reach, trail, keep


def unit_lower_inverse(lower):
    square = lower.shape
    row, col = place(square, 0), place(square, 1)
    apart = row ^ col
    inverse = jnp.where(row == col, 1.0, jnp.where(apart == 1, -lower, 0.0))
    level = 1
    while (1 << level) < square[0]:
        part = jnp.where((apart >> level) == 1, lower, 0.0)
        pair = split(inverse)
        inverse = inverse - dot3(pair, dot3(part, pair))
        level += 1
    return inverse


def activations(proj_ref, before_ref, conv_ref, docs, doc_before, head):
    base = head * HEADW
    rows = proj_ref[:, base : base + CONVW]
    before = before_ref[:, base : base + CONVW]
    taps = conv_ref[:, head * CONVW : (head + 1) * CONVW]
    parts = conv_parts(before, rows, doc_before, docs)
    pre = sum(parts[s] * taps[s : s + 1] for s in range(4))
    gate = sigmoid(pre)
    post = pre * gate
    q_raw, k_raw, value = post[:, :DK], post[:, DK : 2 * DK], post[:, 2 * DK :]
    q_scale = lax.rsqrt(jnp.sum(q_raw * q_raw, axis=-1, keepdims=True) + EPSILON)
    k_scale = lax.rsqrt(jnp.sum(k_raw * k_raw, axis=-1, keepdims=True) + EPSILON)
    query = q_raw * q_scale * DK ** (-0.5)
    key = k_raw * k_scale
    return parts, taps, pre, gate, q_raw, k_raw, q_scale, k_scale, query, key, value


def doc_context(doc_ref, doc_before_ref, chunk):
    docs = doc_ref[...]
    doc_before = jnp.where(chunk > 0, doc_before_ref[...], -1.0)
    return docs, jnp.transpose(docs), doc_before, doc_before[-1:, :]


def forward_kernel(
    heads, proj_ref, before_ref, doc_ref, doc_before_ref, conv_ref, vec_ref, gain_ref,
    gated_ref, recur_ref, inverse_ref, solved_ref, mix_ref, key_ref, tilde_ref, start_ref, state,
):
    chunk = pl.program_id(0)

    @pl.when(chunk == 0)
    def _():
        state[...] = jnp.zeros_like(state)

    docs, doc_row, doc_before, doc_carried = doc_context(doc_ref, doc_before_ref, chunk)
    pair = proj_ref[:, heads * HEADW :]
    decay = -vec_ref[0:1, :] * softplus(pair + vec_ref[1:2, :])
    write = sigmoid(pair)
    cum = cumulate(decay)
    eye = place(docs.shape, 0) == place(docs.shape, 1)
    for head in range(heads):
        acts = activations(proj_ref, before_ref, conv_ref, docs, doc_before, head)
        query, key, value = acts[8:]
        fade, strict, reach, trail, keep = head_decay(cum, 2 * head, docs, doc_row, doc_carried)
        beta = write[:, 2 * head + 1 : 2 * head + 2]
        key_pair = split(key)
        both = dot3(jnp.concatenate([key, query], axis=0), key_pair, NT)
        key_key = both[:CHUNK] * strict
        mix = both[CHUNK:] * fade
        inverse = unit_lower_inverse(beta * key_key)
        rhs = jnp.concatenate([beta * reach * key, beta * value], axis=1)
        solved = dot3(inverse, rhs)
        trailing = jnp.transpose(trail * key)
        outer = dot3(jnp.concatenate([trailing, mix], axis=0), solved)
        step = jnp.where(eye, keep, 0.0) - outer[:CHUNK, :DK]
        q_tilde = reach * query - outer[CHUNK:, :DK]
        tilde = jnp.concatenate([step, q_tilde], axis=0)
        start = state[head]
        moved = dot3(tilde, start)
        state[head] = moved[:CHUNK] + outer[:CHUNK, DK:]
        recurrent = moved[CHUNK:] + outer[CHUNK:, DK:]
        inverse_ref[0, head] = inverse
        solved_ref[0, head] = solved
        mix_ref[0, head] = mix
        key_ref[0, head] = key_key
        tilde_ref[0, head] = tilde
        start_ref[0, head] = start
        recur_ref[:, head * DV : (head + 1) * DV] = recurrent
        scale = lax.rsqrt(jnp.mean(recurrent * recurrent, axis=-1, keepdims=True) + EPSILON)
        z = proj_ref[:, head * HEADW + CONVW : (head + 1) * HEADW]
        gated = recurrent * scale * gain_ref[...] * (z * sigmoid(z))
        gated_ref[:, head * DV : (head + 1) * DV] = gated.astype(BF16)


def backward_kernel(
    heads, chunks, proj_ref, before_ref, doc_ref, doc_before_ref, doc_after_ref,
    conv_ref, vec_ref, gain_ref, recur_ref, inverse_ref, solved_ref, mix_ref, key_ref, tilde_ref,
    start_ref, grad_ref,
    d_proj_ref, d_conv_ref, d_vec_ref, d_gain_ref, d_state, d_after,
):
    step_index = pl.program_id(0)
    chunk = chunks - 1 - step_index

    @pl.when(step_index == 0)
    def _():
        d_state[...] = jnp.zeros_like(d_state)
        d_after[...] = jnp.zeros_like(d_after)
        d_conv_ref[...] = jnp.zeros_like(d_conv_ref)
        d_vec_ref[...] = jnp.zeros_like(d_vec_ref)
        d_gain_ref[...] = jnp.zeros_like(d_gain_ref)

    docs, doc_row, doc_before, doc_carried = doc_context(doc_ref, doc_before_ref, chunk)
    tall_docs = jnp.concatenate([docs, doc_after_ref[...]], axis=0)
    pair = proj_ref[:, heads * HEADW :]
    shifted = pair + vec_ref[1:2, :]
    decay = -vec_ref[0:1, :] * softplus(shifted)
    write = sigmoid(pair)
    cum = cumulate(decay)
    lanes = place(docs.shape, 1)
    last_row = place(docs.shape, 0) == CHUNK - 1
    d_cum = jnp.zeros_like(docs)
    d_write = jnp.zeros_like(docs)
    for head in range(heads):
        acts = activations(proj_ref, before_ref, conv_ref, docs, doc_before, head)
        parts, taps, pre, gate, q_raw, k_raw, q_scale, k_scale, query, key, value = acts
        fade, strict, reach, trail, keep = head_decay(cum, 2 * head, docs, doc_row, doc_carried)
        beta = write[:, 2 * head + 1 : 2 * head + 2]
        grad = grad_ref[:, head * DV : (head + 1) * DV].astype(F32)
        recurrent = recur_ref[:, head * DV : (head + 1) * DV]
        scale = lax.rsqrt(jnp.mean(recurrent * recurrent, axis=-1, keepdims=True) + EPSILON)
        z = proj_ref[:, head * HEADW + CONVW : (head + 1) * HEADW]
        z_gate = sigmoid(z)
        unit = recurrent * scale
        gain = gain_ref[...]
        d_normed = grad * (z * z_gate)
        d_z = grad * unit * gain * (z_gate * (1.0 + z * (1.0 - z_gate)))
        d_gain_ref[...] += jnp.sum(d_normed * unit, axis=0, keepdims=True)
        weighted = d_normed * gain
        d_out = scale * (weighted - unit * jnp.mean(weighted * unit, axis=-1, keepdims=True))
        inverse = inverse_ref[0, head]
        solved = solved_ref[0, head]
        mix = mix_ref[0, head]
        key_key = key_ref[0, head]
        tilde = tilde_ref[0, head]
        start = start_ref[0, head]
        d_next = d_state[head]
        flow = jnp.concatenate([d_next, d_out], axis=0)
        d_state[head] = dot3(tilde, flow, TN)
        start_pair = split(start)
        delta = solved[:, DK:] - dot3(solved[:, :DK], start_pair)
        trailing = trail * key
        d_delta = dot3(jnp.concatenate([trailing, jnp.transpose(mix)], axis=1), flow)
        d_rhs = dot3(inverse, d_delta, TN)
        grads = jnp.concatenate([d_out, d_rhs], axis=0)
        outer = dot3(grads, delta, NT)
        onto = dot3(grads, start_pair, NT)
        d_mix = outer[:CHUNK]
        d_lower = -outer[CHUNK:]
        from_next = dot3(delta, d_next, NT)
        mixed = d_mix * fade
        lowered = d_lower * strict * beta
        d_query = reach * onto[:CHUNK] + dot3(mixed, key)
        d_key = (
            dot3(jnp.transpose(mixed), query)
            + dot3(lowered + jnp.transpose(lowered), key)
            + trail * from_next
            - beta * reach * onto[CHUNK:]
        )
        d_value = beta * d_rhs
        crossed = d_lower * key_key
        net = d_mix * mix + beta * crossed
        reach_col = reach[:, :1]
        sum_query = jnp.sum(query * onto[:CHUNK], axis=-1, keepdims=True)
        sum_key = jnp.sum(key * onto[CHUNK:], axis=-1, keepdims=True)
        sum_trail = jnp.sum(trailing * from_next, axis=-1, keepdims=True)
        d_beta = (
            jnp.sum(crossed, axis=-1, keepdims=True)
            + jnp.sum(d_rhs * value, axis=-1, keepdims=True)
            - reach_col * sum_key
        )
        d_g = (
            jnp.sum(net - jnp.transpose(net), axis=-1, keepdims=True)
            + reach_col * sum_query
            - beta * reach_col * sum_key
            - sum_trail
        )
        kept = keep[:, :1] * jnp.sum(
            jnp.sum(start * d_next, axis=-1, keepdims=True), axis=0, keepdims=True
        )
        d_last = jnp.sum(sum_trail, axis=0, keepdims=True) + kept
        d_g = d_g + jnp.where(last_row[:, :1], d_last, 0.0)
        d_cum = jnp.where(lanes == 2 * head, d_g, d_cum)
        d_write = jnp.where(lanes == 2 * head + 1, d_beta, d_write)
        d_q_raw = (
            (d_query - q_raw * (q_scale * q_scale) * jnp.sum(d_query * q_raw, axis=-1, keepdims=True))
            * q_scale * DK ** (-0.5)
        )
        d_k_raw = (
            d_key - k_raw * (k_scale * k_scale) * jnp.sum(d_key * k_raw, axis=-1, keepdims=True)
        ) * k_scale
        d_post = jnp.concatenate([d_q_raw, d_k_raw, d_value], axis=1)
        d_pre = d_post * gate * (1.0 + pre * (1.0 - gate))
        columns = slice(head * CONVW, (head + 1) * CONVW)
        d_conv_ref[:, columns] += jnp.concatenate(
            [jnp.sum(d_pre * parts[s], axis=0, keepdims=True) for s in range(4)], axis=0
        )
        tall = jnp.concatenate([d_pre, d_after[:, columns]], axis=0)
        d_rows = d_pre * taps[0:1]
        for offset in range(1, 4):
            same = tall_docs[offset : offset + CHUNK, :1] == docs[:, :1]
            d_rows = d_rows + jnp.where(
                same, tall[offset : offset + CHUNK] * taps[offset : offset + 1], 0.0
            )
        d_after[:, columns] = d_pre[:8]
        d_proj_ref[:, head * HEADW : head * HEADW + CONVW] = d_rows.astype(BF16)
        d_proj_ref[:, head * HEADW + CONVW : (head + 1) * HEADW] = d_z.astype(BF16)
    d_decay = cumulate(d_cum, backwards=True)
    d_shifted = d_decay * -vec_ref[0:1, :] * sigmoid(shifted)
    d_written = d_write * write * (1.0 - write)
    used = lanes < 2 * heads
    even = (lanes & 1) == 0
    d_proj_ref[:, heads * HEADW :] = jnp.where(used, jnp.where(even, d_shifted, d_written), 0.0).astype(BF16)
    d_vec_ref[0:1, :] += jnp.sum(d_decay * decay, axis=0, keepdims=True)
    d_vec_ref[1:2, :] += jnp.sum(d_shifted, axis=0, keepdims=True)


def chunk_specs(heads, chunks, where):
    per8 = CHUNK // 8

    def rows(width):
        return pl.BlockSpec((CHUNK, width), lambda c: (where(c), 0))

    def before(width):
        return pl.BlockSpec((8, width), lambda c: (jnp.maximum(where(c) * per8 - 1, 0), 0))

    def after(width):
        return pl.BlockSpec(
            (8, width), lambda c: (jnp.minimum((where(c) + 1) * per8, chunks * per8 - 1), 0)
        )

    def whole(shape):
        return pl.BlockSpec(shape, lambda c: (0,) * len(shape))

    def saved(height, width):
        return pl.BlockSpec((1, heads, height, width), lambda c: (where(c), 0, 0, 0))

    return rows, before, after, whole, saved


def saved_shapes(heads, chunks):
    sizes = ((CHUNK, CHUNK), (CHUNK, DK + DV), (CHUNK, CHUNK), (CHUNK, CHUNK), (2 * CHUNK, DK), (DK, DV))
    return sizes


def mixer_forward(projected, docs, taps, vectors, gain, interpret=False):
    length, width = projected.shape
    heads = (width - CHUNK) // HEADW
    chunks = length // CHUNK
    rows, before, after, whole, saved = chunk_specs(heads, chunks, lambda c: c)
    sizes = saved_shapes(heads, chunks)
    return pl.pallas_call(
        functools.partial(forward_kernel, heads),
        grid=(chunks,),
        in_specs=[
            rows(width), before(width), rows(CHUNK), before(CHUNK),
            whole((4, heads * CONVW)), whole((8, CHUNK)), whole((1, DV)),
        ],
        out_specs=[rows(heads * DV), rows(heads * DV)] + [saved(*s) for s in sizes],
        out_shape=[
            jax.ShapeDtypeStruct((length, heads * DV), BF16),
            jax.ShapeDtypeStruct((length, heads * DV), F32),
        ]
        + [jax.ShapeDtypeStruct((chunks, heads) + s, F32) for s in sizes],
        scratch_shapes=[pltpu.VMEM((heads, DK, DV), F32)],
        name="mixer_forward",
        interpret=interpret,
    )(projected, projected, docs, docs, taps, vectors, gain)


def mixer_backward(projected, docs, taps, vectors, gain, kept, grad, interpret=False):
    length, width = projected.shape
    heads = (width - CHUNK) // HEADW
    chunks = length // CHUNK
    rows, before, after, whole, saved = chunk_specs(heads, chunks, lambda c: chunks - 1 - c)
    sizes = saved_shapes(heads, chunks)
    return pl.pallas_call(
        functools.partial(backward_kernel, heads, chunks),
        grid=(chunks,),
        in_specs=[
            rows(width), before(width), rows(CHUNK), before(CHUNK), after(CHUNK),
            whole((4, heads * CONVW)), whole((8, CHUNK)), whole((1, DV)), rows(heads * DV),
        ]
        + [saved(*s) for s in sizes]
        + [rows(heads * DV)],
        out_specs=[
            rows(width), whole((4, heads * CONVW)), whole((8, CHUNK)), whole((1, DV)),
        ],
        out_shape=[
            jax.ShapeDtypeStruct((length, width), BF16),
            jax.ShapeDtypeStruct((4, heads * CONVW), F32),
            jax.ShapeDtypeStruct((8, CHUNK), F32),
            jax.ShapeDtypeStruct((1, DV), F32),
        ],
        scratch_shapes=[pltpu.VMEM((heads, DK, DV), F32), pltpu.VMEM((8, heads * CONVW), F32)],
        name="mixer_backward",
        interpret=interpret,
    )(projected, projected, docs, docs, docs, taps, vectors, gain, *kept, grad)


def times_transposed(left, right):
    return lax.dot_general(left, right, NT, preferred_element_type=F32)


def transposed_times(left, right):
    return lax.dot_general(left, right, TN, preferred_element_type=F32)


def times(left, right):
    return lax.dot_general(left, right, NN, preferred_element_type=F32)


def block_source(me_ref, place_index, width):
    return pl.ds(pl.multiple_of((me_ref[0] ^ place_index) * width, width), width)


def row_scale(values):
    return lax.rsqrt(jnp.mean(values * values, axis=-1, keepdims=True) + EPSILON)


def prepare_kernel(
    me_ref, x_ref, cot_ref, gain_in_ref, gain_ffn_ref,
    x_out, cot_out, normed_out, gain_in_out, gain_ffn_out,
):
    scale = row_scale(x_ref[...].astype(F32))
    for p in range(x_ref.shape[1] // CHUNK):
        here, source = pl.ds(p * CHUNK, CHUNK), block_source(me_ref, p, CHUNK)
        part = x_ref[:, source]
        gain = gain_in_ref[:, source]
        x_out[:, here] = part
        cot_out[:, here] = cot_ref[:, source]
        normed_out[:, here] = (part.astype(F32) * scale * gain).astype(BF16)
        gain_in_out[:, here] = gain
        gain_ffn_out[:, here] = gain_ffn_ref[:, source]


def middle_kernel(x_ref, mixed_ref, gain_ref, resid_out, normed_out):
    resid = x_ref[...].astype(F32) + mixed_ref[...].astype(F32)
    resid_out[...] = resid
    normed_out[...] = (resid * row_scale(resid) * gain_ref[...]).astype(BF16)


def ffn_back_kernel(me_ref, resid_ref, cot_ref, grad_ref, gain_ref, d_resid_out, d_mixed_out, d_gain_out):
    resid = resid_ref[...]
    grad = grad_ref[...].astype(F32)
    scale = row_scale(resid)
    unit = resid * scale
    weighted = grad * gain_ref[...]
    inner = jnp.mean(weighted * unit, axis=-1, keepdims=True)
    d_resid = cot_ref[...].astype(F32) + scale * (weighted - unit * inner)
    d_resid_out[...] = d_resid
    d_mixed_out[...] = d_resid.astype(BF16)
    sums = jnp.sum(grad * unit, axis=0, keepdims=True)
    for p in range(resid.shape[1] // CHUNK):
        d_gain_out[:, block_source(me_ref, p, CHUNK)] = sums[:, p * CHUNK : (p + 1) * CHUNK]


def output_kernel(me_ref, resid_ref, ffn_ref, out_ref):
    for p in range(resid_ref.shape[1] // CHUNK):
        here = pl.ds(p * CHUNK, CHUNK)
        total = resid_ref[:, here] + ffn_ref[:, here].astype(F32)
        out_ref[:, block_source(me_ref, p, CHUNK)] = total.astype(BF16)


def gain_kernel(me_ref, grad_ref, normed_ref, gain_ref, out_ref):
    sums = jnp.sum(grad_ref[...].astype(F32) * normed_ref[...].astype(F32), axis=0, keepdims=True)
    sums = sums / gain_ref[...]
    for p in range(grad_ref.shape[1] // CHUNK):
        out_ref[:, block_source(me_ref, p, CHUNK)] = sums[:, p * CHUNK : (p + 1) * CHUNK]


def finish_kernel(me_ref, x_ref, d_resid_ref, grad_ref, gain_ref, out_ref):
    x = x_ref[...].astype(F32)
    scale = row_scale(x)
    unit = x * scale
    weighted = grad_ref[...].astype(F32) * gain_ref[...]
    inner = jnp.mean(weighted * unit, axis=-1, keepdims=True)
    total = d_resid_ref[...] + scale * (weighted - unit * inner)
    for p in range(x.shape[1] // CHUNK):
        out_ref[:, block_source(me_ref, p, CHUNK)] = total[:, p * CHUNK : (p + 1) * CHUNK]


def row_call(kernel, name, outs, *args):
    def space(arg):
        kind = pltpu.SMEM if arg.dtype == jnp.int32 else pltpu.VMEM
        return pl.BlockSpec(memory_space=kind)

    return pl.pallas_call(
        kernel,
        in_specs=[space(a) for a in args],
        out_specs=[pl.BlockSpec(memory_space=pltpu.VMEM)] * len(outs),
        out_shape=[jax.ShapeDtypeStruct(s, d) for s, d in outs],
        name=name,
    )(*args)


def swap(value, axis, mask):
    pairs = [(i, i ^ mask) for i in range(lax.axis_size(axis))]
    return lax.ppermute(value, axis, pairs)


def small_dp():
    return lax.axis_size("dp") == 8


def gather_pieces(own):
    across = [own] + [swap(own, "dp", 2 * q) for q in range(1, 4)]
    beside = [swap(piece, "dp", 1) for piece in across]
    return [piece for pair in zip(across, beside) for piece in pair]


def gather_dp(own, axis):
    if small_dp():
        return jnp.concatenate(gather_pieces(own), axis=axis)
    return lax.all_gather(own, "dp", axis=axis, tiled=True)


def scatter_dp(partial, axis):
    if not small_dp():
        return lax.psum_scatter(partial, "dp", scatter_dimension=axis, tiled=True).astype(F32)
    blocks = jnp.split(partial, 8, axis=axis)
    sent = swap(jnp.concatenate(blocks[1::2], axis=axis), "dp", 1)
    halves = [
        (mine.astype(F32) + other.astype(F32)).astype(BF16)
        for mine, other in zip(blocks[0::2], jnp.split(sent, 4, axis=axis))
    ]
    total = halves[0].astype(F32)
    for q in range(1, 4):
        total = total + swap(halves[q], "dp", 2 * q).astype(F32)
    return total


def tree_sum(value, axis):
    parts = [value] + [swap(value, axis, mask) for mask in range(1, lax.axis_size(axis))]
    while len(parts) > 1:
        parts = [left + right for left, right in zip(parts[0::2], parts[1::2])]
    return parts[0]


def after(value, anchor):
    return lax.optimization_barrier((value, anchor))[0]


def local(
    inputs,
    segments,
    cotangent,
    norm_in,
    w_in,
    w_alpha_beta,
    conv_weight,
    a_log,
    dt_bias,
    out_gain,
    w_out,
    norm_ffn,
    w_gate,
    w_up,
    w_down,
):
    doc_ids = segments[0]
    length = doc_ids.shape[0]
    rows, features = inputs.shape
    part_index = lax.axis_index("tensor")
    parts = lax.axis_size("tensor")
    head_count = a_log.shape[0] // parts
    conv_width = head_count * CONVW
    hidden_units = w_down.shape[0]
    order = lax.axis_index("dp") if small_dp() else jnp.zeros((), jnp.int32)
    me = order.astype(jnp.int32)[None]
    conv_mine = lax.dynamic_slice_in_dim(conv_weight, part_index * conv_width, conv_width, 1)
    alog_mine = lax.dynamic_slice_in_dim(a_log, part_index * head_count, head_count, 0)
    bias_mine = lax.dynamic_slice_in_dim(dt_bias, part_index * head_count, head_count, 0)
    docs = jnp.broadcast_to(doc_ids.astype(F32)[:, None], (length, CHUNK))
    lane_pair = jnp.stack([jnp.exp(alog_mine), bias_mine])
    spread = jnp.stack([lane_pair, jnp.zeros_like(lane_pair)], axis=-1).reshape(2, 2 * head_count)
    vectors = jnp.pad(spread, ((0, 6), (0, CHUNK - 2 * head_count)))
    gain_row = out_gain[None, :]

    token_bf, token_f32 = ((rows, features), BF16), ((rows, features), F32)
    gain_shape = ((1, features), F32)
    x, cot, normed, gain_in, gain_ffn = row_call(
        prepare_kernel, "prepare", [token_bf, token_bf, token_bf, gain_shape, gain_shape],
        me, inputs, cotangent, norm_in[None], norm_ffn[None],
    )
    joined = jnp.concatenate(
        [w_in, jnp.pad(w_alpha_beta, ((0, 0), (0, CHUNK - w_alpha_beta.shape[1])))], axis=1
    )
    seq_rows = lax.all_gather(normed, "tensor", axis=0, tiled=True)
    whole_in = gather_dp(joined, 0)
    unit_weights = jnp.concatenate([w_gate.T, w_up.T, w_down, w_out], axis=0)
    whole_units = gather_dp(after(unit_weights, whole_in), 1)
    whole_pre = whole_units[: 2 * hidden_units]
    whole_down = whole_units[2 * hidden_units : 3 * hidden_units]
    whole_out = whole_units[3 * hidden_units :]
    projected = times(seq_rows, whole_in)
    back_seq = lax.all_gather(after(cot, seq_rows), "tensor", axis=0, tiled=True)
    gated, *kept = mixer_forward(projected, docs, conv_mine, vectors, gain_row)
    mixed = lax.psum_scatter(
        times(gated, whole_out).astype(BF16), "tensor", scatter_dimension=0, tiled=True
    )
    resid, normed_ffn = row_call(middle_kernel, "middle", [token_f32, token_bf], x, mixed, gain_ffn)

    ffn_seq = lax.all_gather(normed_ffn, "tensor", axis=0, tiled=True)
    pre = times_transposed(whole_pre, ffn_seq)
    gate_pre, up_pre = pre[:hidden_units], pre[hidden_units:]
    d_hidden = times_transposed(whole_down, back_seq)
    sig = jax.nn.sigmoid(gate_pre)
    hidden = (gate_pre * sig * up_pre).astype(BF16)
    d_up = (d_hidden * gate_pre * sig).astype(BF16)
    d_gate = (d_hidden * up_pre * sig * (1.0 + gate_pre * (1.0 - sig))).astype(BF16)
    d_pre = jnp.concatenate([d_gate, d_up], axis=0)
    d_normed_ffn = lax.psum_scatter(
        transposed_times(d_pre, whole_pre).astype(BF16), "tensor", scatter_dimension=0, tiled=True
    )
    grad_pre = scatter_dp(times(d_pre, ffn_seq).astype(BF16), 1)
    grad_down = scatter_dp(times(hidden, back_seq).astype(BF16), 1)
    d_resid, d_mixed, gain_ffn_part = row_call(
        ffn_back_kernel, "ffn_back", [token_f32, token_bf, gain_shape],
        me, resid, cot, d_normed_ffn, gain_ffn,
    )

    mixer_back_seq = lax.all_gather(d_mixed, "tensor", axis=0, tiled=True)
    ffn_part = after(transposed_times(hidden, whole_down).astype(BF16), mixer_back_seq)
    ffn_out = lax.psum_scatter(ffn_part, "tensor", scatter_dimension=0, tiled=True)
    (output,) = row_call(output_kernel, "output", [token_bf], me, resid, ffn_out)
    d_gated = times_transposed(mixer_back_seq, whole_out)
    grad_out = scatter_dp(transposed_times(gated, mixer_back_seq).astype(BF16), 1)
    d_projected, d_conv, d_vectors, d_gain_out = mixer_backward(
        projected, docs, conv_mine, vectors, gain_row, kept, d_gated
    )
    d_part = times_transposed(d_projected, whole_in).astype(BF16)
    d_normed_in = lax.psum_scatter(d_part, "tensor", scatter_dimension=0, tiled=True)
    grad_joined = scatter_dp(transposed_times(seq_rows, d_projected).astype(BF16), 0)
    (gain_in_part,) = row_call(gain_kernel, "gain", [gain_shape], me, d_part, seq_rows, gain_in)
    (d_inputs,) = row_call(
        finish_kernel, "finish", [token_f32], me, x, d_resid, d_normed_in, gain_in
    )

    last = jnp.concatenate(
        [
            d_gain_out,
            d_vectors[:1, : 2 * head_count],
            d_vectors[1:2, : 2 * head_count],
        ],
        axis=1,
    )
    last = jnp.pad(last, ((0, 0), (0, conv_width - last.shape[1])))
    if conv_width == features:
        table = jnp.concatenate([d_conv, gain_in_part, gain_ffn_part, last], axis=0)
        table = tree_sum(table, "dp") if small_dp() else lax.psum(table, "dp")
        tables = [table] + [swap(table, "tensor", mask) for mask in range(1, parts)]
    else:
        raise ValueError("conv width")
    shared = [t[4:] for t in tables]
    while len(shared) > 1:
        shared = [left + right for left, right in zip(shared[0::2], shared[1::2])]
    shared = shared[0]
    grad_conv = jnp.zeros(conv_weight.shape, F32)
    own = jnp.zeros((2, a_log.shape[0]), F32)
    width = out_gain.shape[0]
    for mask, t in enumerate(tables):
        place_index = part_index ^ mask
        grad_conv = lax.dynamic_update_slice_in_dim(grad_conv, t[:4], place_index * conv_width, 1)
        pair = t[6, width : width + 4 * head_count].reshape(2, 2 * head_count)[:, ::2]
        own = lax.dynamic_update_slice_in_dim(own, pair, place_index * head_count, 1)
    columns = w_in.shape[1]
    return (
        output,
        d_inputs,
        shared[0],
        grad_joined[:, :columns],
        grad_joined[:, columns : columns + w_alpha_beta.shape[1]],
        grad_conv,
        own[0],
        own[1],
        shared[2, :width],
        grad_out,
        shared[1],
        grad_pre[:hidden_units].T,
        grad_pre[hidden_units:].T,
        grad_down,
    )


def solution(mesh):
    return jax.shard_map(
        local,
        mesh=mesh,
        in_specs=(
            P(("dp", "tensor"), None),
            P("dp", None),
            P(("dp", "tensor"), None),
            P(),
            P("dp", "tensor"),
            P("dp", "tensor"),
            P(),
            P(),
            P(),
            P(),
            P("tensor", "dp"),
            P(),
            P("dp", "tensor"),
            P("dp", "tensor"),
            P("tensor", "dp"),
        ),
        out_specs=(
            P(("dp", "tensor"), None),
            P(("dp", "tensor"), None),
            P(),
            P("dp", "tensor"),
            P("dp", "tensor"),
            P(),
            P(),
            P(),
            P(),
            P("tensor", "dp"),
            P(),
            P("dp", "tensor"),
            P("dp", "tensor"),
            P("tensor", "dp"),
        ),
        check_vma=False,
    )
```

```python
import functools
import jax
import jax.numpy as jnp
from jax import lax
from jax.experimental import pallas as pl
from jax.experimental.pallas import tpu as pltpu

from jax.sharding import PartitionSpec as P

DK = 128
DV = 256
CONVW = 2 * DK + DV
HEADW = 2 * DK + 2 * DV
CHUNK = 128
EPSILON = 1e-06
F32 = jnp.float32
BF16 = jnp.bfloat16
NN = (((1,), (0,)), ((), ()))
NT = (((1,), (1,)), ((), ()))
TN = (((0,), (0,)), ((), ()))


def split(value):
    high = value.astype(BF16)
    return high, (value - high.astype(F32)).astype(BF16)


def dot3(left, right, dims=NN):
    lh, ll = left if isinstance(left, tuple) else split(left)
    rh, rl = right if isinstance(right, tuple) else split(right)
    d = functools.partial(lax.dot_general, dimension_numbers=dims, preferred_element_type=F32)
    return d(lh, rh) + (d(lh, rl) + d(ll, rh))


def sigmoid(x):
    return 1.0 / (1.0 + jnp.exp(-x))


def softplus(x):
    return jnp.maximum(x, 0.0) + jnp.log(1.0 + jnp.exp(-jnp.abs(x)))


def place(shape, axis):
    return lax.broadcasted_iota(jnp.int32, shape, axis)


def cumulate(value, backwards=False):
    length = value.shape[0]
    row = place(value.shape, 0)
    step = 1
    while step < length:
        if backwards:
            moved = pltpu.roll(value, length - step, 0)
            value = value + jnp.where(row < length - step, moved, 0.0)
        else:
            moved = pltpu.roll(value, step, 0)
            value = value + jnp.where(row >= step, moved, 0.0)
        step *= 2
    return value


def conv_parts(before, rows, doc_before, docs):
    length = rows.shape[0]
    tall = jnp.concatenate([before, rows], axis=0)
    tall_docs = jnp.concatenate([doc_before, docs], axis=0)
    parts = [rows]
    for offset in range(1, 4):
        same = tall_docs[8 - offset : 8 - offset + length, :1] == docs[:, :1]
        parts.append(jnp.where(same, tall[8 - offset : 8 - offset + length], 0.0))
    return parts


def head_decay(cum, lane, docs, doc_row, doc_carried):
    square = docs.shape
    g_col = jnp.broadcast_to(cum[:, lane : lane + 1], square)
    g_row = jnp.transpose(g_col)
    row, col = place(square, 0), place(square, 1)
    seen = (row >= col) & (docs == doc_row)
    fade = jnp.where(seen, jnp.exp(jnp.where(seen, g_col - g_row, 0.0)), 0.0)
    strict = jnp.where(row > col, fade, 0.0)
    reach = jnp.where(docs == doc_carried, jnp.exp(g_col), 0.0)
    g_last = g_col[-1:, :]
    doc_last = docs[-1:, :]
    trail = jnp.where(docs == doc_last, jnp.exp(g_last - g_col), 0.0)
    keep = jnp.where(doc_last == doc_carried, jnp.exp(g_last), 0.0)
    return fade, strict, reach, trail, keep


def unit_lower_inverse(lower):
    square = lower.shape
    row, col = place(square, 0), place(square, 1)
    apart = row ^ col
    inverse = jnp.where(row == col, 1.0, jnp.where(apart == 1, -lower, 0.0))
    level = 1
    while (1 << level) < square[0]:
        part = jnp.where((apart >> level) == 1, lower, 0.0)
        pair = split(inverse)
        inverse = inverse - dot3(pair, dot3(part, pair))
        level += 1
    return inverse


def activations(proj_ref, before_ref, conv_ref, docs, doc_before, head):
    base = head * HEADW
    rows = proj_ref[:, base : base + CONVW]
    before = before_ref[:, base : base + CONVW]
    taps = conv_ref[:, head * CONVW : (head + 1) * CONVW]
    parts = conv_parts(before, rows, doc_before, docs)
    pre = sum(parts[s] * taps[s : s + 1] for s in range(4))
    gate = sigmoid(pre)
    post = pre * gate
    q_raw, k_raw, value = post[:, :DK], post[:, DK : 2 * DK], post[:, 2 * DK :]
    q_scale = lax.rsqrt(jnp.sum(q_raw * q_raw, axis=-1, keepdims=True) + EPSILON)
    k_scale = lax.rsqrt(jnp.sum(k_raw * k_raw, axis=-1, keepdims=True) + EPSILON)
    query = q_raw * q_scale * DK ** (-0.5)
    key = k_raw * k_scale
    return parts, taps, pre, gate, q_raw, k_raw, q_scale, k_scale, query, key, value


def doc_context(doc_ref, doc_before_ref, chunk):
    docs = doc_ref[...]
    doc_before = jnp.where(chunk > 0, doc_before_ref[...], -1.0)
    return docs, jnp.transpose(docs), doc_before, doc_before[-1:, :]


def forward_kernel(
    heads, proj_ref, before_ref, doc_ref, doc_before_ref, conv_ref, vec_ref, gain_ref,
    gated_ref, recur_ref, inverse_ref, solved_ref, mix_ref, key_ref, tilde_ref, start_ref, state,
):
    chunk = pl.program_id(0)

    @pl.when(chunk == 0)
    def _():
        state[...] = jnp.zeros_like(state)

    docs, doc_row, doc_before, doc_carried = doc_context(doc_ref, doc_before_ref, chunk)
    pair = proj_ref[:, heads * HEADW :]
    decay = -vec_ref[0:1, :] * softplus(pair + vec_ref[1:2, :])
    write = sigmoid(pair)
    cum = cumulate(decay)
    eye = place(docs.shape, 0) == place(docs.shape, 1)
    for head in range(heads):
        acts = activations(proj_ref, before_ref, conv_ref, docs, doc_before, head)
        query, key, value = acts[8:]
        fade, strict, reach, trail, keep = head_decay(cum, 2 * head, docs, doc_row, doc_carried)
        beta = write[:, 2 * head + 1 : 2 * head + 2]
        key_pair = split(key)
        both = dot3(jnp.concatenate([key, query], axis=0), key_pair, NT)
        key_key = both[:CHUNK] * strict
        mix = both[CHUNK:] * fade
        inverse = unit_lower_inverse(beta * key_key)
        rhs = jnp.concatenate([beta * reach * key, beta * value], axis=1)
        solved = dot3(inverse, rhs)
        trailing = jnp.transpose(trail * key)
        outer = dot3(jnp.concatenate([trailing, mix], axis=0), solved)
        step = jnp.where(eye, keep, 0.0) - outer[:CHUNK, :DK]
        q_tilde = reach * query - outer[CHUNK:, :DK]
        tilde = jnp.concatenate([step, q_tilde], axis=0)
        start = state[head]
        moved = dot3(tilde, start)
        state[head] = moved[:CHUNK] + outer[:CHUNK, DK:]
        recurrent = moved[CHUNK:] + outer[CHUNK:, DK:]
        inverse_ref[0, head] = inverse
        solved_ref[0, head] = solved
        mix_ref[0, head] = mix
        key_ref[0, head] = key_key
        tilde_ref[0, head] = tilde
        start_ref[0, head] = start
        recur_ref[:, head * DV : (head + 1) * DV] = recurrent
        scale = lax.rsqrt(jnp.mean(recurrent * recurrent, axis=-1, keepdims=True) + EPSILON)
        z = proj_ref[:, head * HEADW + CONVW : (head + 1) * HEADW]
        gated = recurrent * scale * gain_ref[...] * (z * sigmoid(z))
        gated_ref[:, head * DV : (head + 1) * DV] = gated.astype(BF16)


def backward_kernel(
    heads, chunks, proj_ref, before_ref, doc_ref, doc_before_ref, doc_after_ref,
    conv_ref, vec_ref, gain_ref, recur_ref, inverse_ref, solved_ref, mix_ref, key_ref, tilde_ref,
    start_ref, grad_ref,
    d_proj_ref, d_conv_ref, d_vec_ref, d_gain_ref, d_state, d_after,
):
    step_index = pl.program_id(0)
    chunk = chunks - 1 - step_index

    @pl.when(step_index == 0)
    def _():
        d_state[...] = jnp.zeros_like(d_state)
        d_after[...] = jnp.zeros_like(d_after)
        d_conv_ref[...] = jnp.zeros_like(d_conv_ref)
        d_vec_ref[...] = jnp.zeros_like(d_vec_ref)
        d_gain_ref[...] = jnp.zeros_like(d_gain_ref)

    docs, doc_row, doc_before, doc_carried = doc_context(doc_ref, doc_before_ref, chunk)
    tall_docs = jnp.concatenate([docs, doc_after_ref[...]], axis=0)
    pair = proj_ref[:, heads * HEADW :]
    shifted = pair + vec_ref[1:2, :]
    decay = -vec_ref[0:1, :] * softplus(shifted)
    write = sigmoid(pair)
    cum = cumulate(decay)
    lanes = place(docs.shape, 1)
    last_row = place(docs.shape, 0) == CHUNK - 1
    d_cum = jnp.zeros_like(docs)
    d_write = jnp.zeros_like(docs)
    for head in range(heads):
        acts = activations(proj_ref, before_ref, conv_ref, docs, doc_before, head)
        parts, taps, pre, gate, q_raw, k_raw, q_scale, k_scale, query, key, value = acts
        fade, strict, reach, trail, keep = head_decay(cum, 2 * head, docs, doc_row, doc_carried)
        beta = write[:, 2 * head + 1 : 2 * head + 2]
        grad = grad_ref[:, head * DV : (head + 1) * DV].astype(F32)
        recurrent = recur_ref[:, head * DV : (head + 1) * DV]
        scale = lax.rsqrt(jnp.mean(recurrent * recurrent, axis=-1, keepdims=True) + EPSILON)
        z = proj_ref[:, head * HEADW + CONVW : (head + 1) * HEADW]
        z_gate = sigmoid(z)
        unit = recurrent * scale
        gain = gain_ref[...]
        d_normed = grad * (z * z_gate)
        d_z = grad * unit * gain * (z_gate * (1.0 + z * (1.0 - z_gate)))
        d_gain_ref[...] += jnp.sum(d_normed * unit, axis=0, keepdims=True)
        weighted = d_normed * gain
        d_out = scale * (weighted - unit * jnp.mean(weighted * unit, axis=-1, keepdims=True))
        inverse = inverse_ref[0, head]
        solved = solved_ref[0, head]
        mix = mix_ref[0, head]
        key_key = key_ref[0, head]
        tilde = tilde_ref[0, head]
        start = start_ref[0, head]
        d_next = d_state[head]
        flow = jnp.concatenate([d_next, d_out], axis=0)
        d_state[head] = dot3(tilde, flow, TN)
        start_pair = split(start)
        delta = solved[:, DK:] - dot3(solved[:, :DK], start_pair)
        trailing = trail * key
        d_delta = dot3(jnp.concatenate([trailing, jnp.transpose(mix)], axis=1), flow)
        d_rhs = dot3(inverse, d_delta, TN)
        grads = jnp.concatenate([d_out, d_rhs], axis=0)
        outer = dot3(grads, delta, NT)
        onto = dot3(grads, start_pair, NT)
        d_mix = outer[:CHUNK]
        d_lower = -outer[CHUNK:]
        from_next = dot3(delta, d_next, NT)
        mixed = d_mix * fade
        lowered = d_lower * strict * beta
        d_query = reach * onto[:CHUNK] + dot3(mixed, key)
        d_key = (
            dot3(jnp.transpose(mixed), query)
            + dot3(lowered + jnp.transpose(lowered), key)
            + trail * from_next
            - beta * reach * onto[CHUNK:]
        )
        d_value = beta * d_rhs
        crossed = d_lower * key_key
        net = d_mix * mix + beta * crossed
        reach_col = reach[:, :1]
        sum_query = jnp.sum(query * onto[:CHUNK], axis=-1, keepdims=True)
        sum_key = jnp.sum(key * onto[CHUNK:], axis=-1, keepdims=True)
        sum_trail = jnp.sum(trailing * from_next, axis=-1, keepdims=True)
        d_beta = (
            jnp.sum(crossed, axis=-1, keepdims=True)
            + jnp.sum(d_rhs * value, axis=-1, keepdims=True)
            - reach_col * sum_key
        )
        d_g = (
            jnp.sum(net - jnp.transpose(net), axis=-1, keepdims=True)
            + reach_col * sum_query
            - beta * reach_col * sum_key
            - sum_trail
        )
        kept = keep[:, :1] * jnp.sum(
            jnp.sum(start * d_next, axis=-1, keepdims=True), axis=0, keepdims=True
        )
        d_last = jnp.sum(sum_trail, axis=0, keepdims=True) + kept
        d_g = d_g + jnp.where(last_row[:, :1], d_last, 0.0)
        d_cum = jnp.where(lanes == 2 * head, d_g, d_cum)
        d_write = jnp.where(lanes == 2 * head + 1, d_beta, d_write)
        d_q_raw = (
            (d_query - q_raw * (q_scale * q_scale) * jnp.sum(d_query * q_raw, axis=-1, keepdims=True))
            * q_scale * DK ** (-0.5)
        )
        d_k_raw = (
            d_key - k_raw * (k_scale * k_scale) * jnp.sum(d_key * k_raw, axis=-1, keepdims=True)
        ) * k_scale
        d_post = jnp.concatenate([d_q_raw, d_k_raw, d_value], axis=1)
        d_pre = d_post * gate * (1.0 + pre * (1.0 - gate))
        columns = slice(head * CONVW, (head + 1) * CONVW)
        d_conv_ref[:, columns] += jnp.concatenate(
            [jnp.sum(d_pre * parts[s], axis=0, keepdims=True) for s in range(4)], axis=0
        )
        tall = jnp.concatenate([d_pre, d_after[:, columns]], axis=0)
        d_rows = d_pre * taps[0:1]
        for offset in range(1, 4):
            same = tall_docs[offset : offset + CHUNK, :1] == docs[:, :1]
            d_rows = d_rows + jnp.where(
                same, tall[offset : offset + CHUNK] * taps[offset : offset + 1], 0.0
            )
        d_after[:, columns] = d_pre[:8]
        d_proj_ref[:, head * HEADW : head * HEADW + CONVW] = d_rows.astype(BF16)
        d_proj_ref[:, head * HEADW + CONVW : (head + 1) * HEADW] = d_z.astype(BF16)
    d_decay = cumulate(d_cum, backwards=True)
    d_shifted = d_decay * -vec_ref[0:1, :] * sigmoid(shifted)
    d_written = d_write * write * (1.0 - write)
    used = lanes < 2 * heads
    even = (lanes & 1) == 0
    d_proj_ref[:, heads * HEADW :] = jnp.where(used, jnp.where(even, d_shifted, d_written), 0.0).astype(BF16)
    d_vec_ref[0:1, :] += jnp.sum(d_decay * decay, axis=0, keepdims=True)
    d_vec_ref[1:2, :] += jnp.sum(d_shifted, axis=0, keepdims=True)


def chunk_specs(heads, chunks, where):
    per8 = CHUNK // 8

    def rows(width):
        return pl.BlockSpec((CHUNK, width), lambda c: (where(c), 0))

    def before(width):
        return pl.BlockSpec((8, width), lambda c: (jnp.maximum(where(c) * per8 - 1, 0), 0))

    def after(width):
        return pl.BlockSpec(
            (8, width), lambda c: (jnp.minimum((where(c) + 1) * per8, chunks * per8 - 1), 0)
        )

    def whole(shape):
        return pl.BlockSpec(shape, lambda c: (0,) * len(shape))

    def saved(height, width):
        return pl.BlockSpec((1, heads, height, width), lambda c: (where(c), 0, 0, 0))

    return rows, before, after, whole, saved


def saved_shapes():
    sizes = ((CHUNK, CHUNK), (CHUNK, DK + DV), (CHUNK, CHUNK), (CHUNK, CHUNK), (2 * CHUNK, DK), (DK, DV))
    return sizes


def mixer_forward(projected, docs, taps, vectors, gain, interpret=False):
    length, width = projected.shape
    heads = (width - CHUNK) // HEADW
    chunks = length // CHUNK
    rows, before, _, whole, saved = chunk_specs(heads, chunks, lambda c: c)
    sizes = saved_shapes()
    return pl.pallas_call(
        functools.partial(forward_kernel, heads),
        grid=(chunks,),
        in_specs=[
            rows(width), before(width), rows(CHUNK), before(CHUNK),
            whole((4, heads * CONVW)), whole((8, CHUNK)), whole((1, DV)),
        ],
        out_specs=[rows(heads * DV), rows(heads * DV)] + [saved(*s) for s in sizes],
        out_shape=[
            jax.ShapeDtypeStruct((length, heads * DV), BF16),
            jax.ShapeDtypeStruct((length, heads * DV), F32),
        ]
        + [jax.ShapeDtypeStruct((chunks, heads) + s, F32) for s in sizes],
        scratch_shapes=[pltpu.VMEM((heads, DK, DV), F32)],
        name="mixer_forward",
        interpret=interpret,
    )(projected, projected, docs, docs, taps, vectors, gain)


def mixer_backward(projected, docs, taps, vectors, gain, kept, grad, interpret=False):
    length, width = projected.shape
    heads = (width - CHUNK) // HEADW
    chunks = length // CHUNK
    rows, before, after, whole, saved = chunk_specs(heads, chunks, lambda c: chunks - 1 - c)
    sizes = saved_shapes()
    return pl.pallas_call(
        functools.partial(backward_kernel, heads, chunks),
        grid=(chunks,),
        in_specs=[
            rows(width), before(width), rows(CHUNK), before(CHUNK), after(CHUNK),
            whole((4, heads * CONVW)), whole((8, CHUNK)), whole((1, DV)), rows(heads * DV),
        ]
        + [saved(*s) for s in sizes]
        + [rows(heads * DV)],
        out_specs=[
            rows(width), whole((4, heads * CONVW)), whole((8, CHUNK)), whole((1, DV)),
        ],
        out_shape=[
            jax.ShapeDtypeStruct((length, width), BF16),
            jax.ShapeDtypeStruct((4, heads * CONVW), F32),
            jax.ShapeDtypeStruct((8, CHUNK), F32),
            jax.ShapeDtypeStruct((1, DV), F32),
        ],
        scratch_shapes=[pltpu.VMEM((heads, DK, DV), F32), pltpu.VMEM((8, heads * CONVW), F32)],
        name="mixer_backward",
        interpret=interpret,
    )(projected, projected, docs, docs, docs, taps, vectors, gain, *kept, grad)


def times_transposed(left, right):
    return lax.dot_general(left, right, NT, preferred_element_type=F32)


def transposed_times(left, right):
    return lax.dot_general(left, right, TN, preferred_element_type=F32)


def times(left, right):
    return lax.dot_general(left, right, NN, preferred_element_type=F32)


def block_source(me_ref, place_index, width):
    return pl.ds(pl.multiple_of((me_ref[0] ^ place_index) * width, width), width)


def row_scale(values):
    return lax.rsqrt(jnp.mean(values * values, axis=-1, keepdims=True) + EPSILON)


def prepare_kernel(
    me_ref, x_ref, cot_ref, gain_in_ref, gain_ffn_ref,
    x_out, cot_out, normed_out, gain_in_out, gain_ffn_out,
):
    scale = row_scale(x_ref[...].astype(F32))
    for p in range(x_ref.shape[1] // CHUNK):
        here, source = pl.ds(p * CHUNK, CHUNK), block_source(me_ref, p, CHUNK)
        part = x_ref[:, source]
        gain = gain_in_ref[:, source]
        x_out[:, here] = part
        cot_out[:, here] = cot_ref[:, source]
        normed_out[:, here] = (part.astype(F32) * scale * gain).astype(BF16)
        gain_in_out[:, here] = gain
        gain_ffn_out[:, here] = gain_ffn_ref[:, source]


def middle_kernel(x_ref, mixed_ref, gain_ref, resid_out, normed_out):
    resid = x_ref[...].astype(F32) + mixed_ref[...].astype(F32)
    resid_out[...] = resid
    normed_out[...] = (resid * row_scale(resid) * gain_ref[...]).astype(BF16)


def ffn_back_kernel(me_ref, resid_ref, cot_ref, grad_ref, mate_ref, gain_ref, d_resid_out, d_mixed_out, d_gain_out):
    resid = resid_ref[...]
    grad = grad_ref[...].astype(F32) + mate_ref[...].astype(F32)
    scale = row_scale(resid)
    unit = resid * scale
    weighted = grad * gain_ref[...]
    inner = jnp.mean(weighted * unit, axis=-1, keepdims=True)
    d_resid = cot_ref[...].astype(F32) + scale * (weighted - unit * inner)
    d_resid_out[...] = d_resid
    d_mixed_out[...] = d_resid.astype(BF16)
    sums = jnp.sum(grad * unit, axis=0, keepdims=True)
    for p in range(resid.shape[1] // CHUNK):
        d_gain_out[:, block_source(me_ref, p, CHUNK)] = sums[:, p * CHUNK : (p + 1) * CHUNK]


def output_kernel(me_ref, resid_ref, own_ref, mate_ref, out_ref):
    for p in range(resid_ref.shape[1] // CHUNK):
        here = pl.ds(p * CHUNK, CHUNK)
        ffn = own_ref[:, here].astype(F32) + mate_ref[:, here].astype(F32)
        total = resid_ref[:, here] + ffn
        out_ref[:, block_source(me_ref, p, CHUNK)] = total.astype(BF16)


def gain_kernel(me_ref, grad_ref, normed_ref, gain_ref, out_ref):
    sums = jnp.sum(grad_ref[...].astype(F32) * normed_ref[...].astype(F32), axis=0, keepdims=True)
    sums = sums / gain_ref[...]
    for p in range(grad_ref.shape[1] // CHUNK):
        out_ref[:, block_source(me_ref, p, CHUNK)] = sums[:, p * CHUNK : (p + 1) * CHUNK]


def finish_kernel(me_ref, x_ref, d_resid_ref, grad_ref, gain_ref, out_ref):
    x = x_ref[...].astype(F32)
    scale = row_scale(x)
    unit = x * scale
    weighted = grad_ref[...].astype(F32) * gain_ref[...]
    inner = jnp.mean(weighted * unit, axis=-1, keepdims=True)
    total = d_resid_ref[...] + scale * (weighted - unit * inner)
    for p in range(x.shape[1] // CHUNK):
        out_ref[:, block_source(me_ref, p, CHUNK)] = total[:, p * CHUNK : (p + 1) * CHUNK]


UNIT_STEPS = 2


def feed_kernel(
    tok_ref, cot_ref, *refs,
):
    weights, outs = (refs[:3], refs[3:6]), (refs[6:9], refs[9:12])
    d_out, y_out, d_total, y_total = refs[12:]
    step = pl.program_id(0)

    @pl.when(step == 0)
    def _():
        d_total[...] = jnp.zeros_like(d_total)
        y_total[...] = jnp.zeros_like(y_total)

    tokens, cots = tok_ref[...], cot_ref[...]
    for (gate_w, up_w, down_w), (gate_out, up_out, hidden_out) in zip(weights, outs):
        gate_pre = times_transposed(gate_w[...], tokens)
        up_pre = times_transposed(up_w[...], tokens)
        d_hidden = times_transposed(down_w[...], cots)
        sig = sigmoid(gate_pre)
        silu = gate_pre * sig
        hidden = (silu * up_pre).astype(BF16)
        d_up = (d_hidden * silu).astype(BF16)
        d_gate = (d_hidden * up_pre * (sig * (1.0 + gate_pre * (1.0 - sig)))).astype(BF16)
        gate_out[...] = d_gate
        up_out[...] = d_up
        hidden_out[...] = hidden
        d_total[...] += transposed_times(d_gate, gate_w[...]) + transposed_times(d_up, up_w[...])
        y_total[...] += transposed_times(hidden, down_w[...])

    @pl.when(step == UNIT_STEPS - 1)
    def _():
        d_out[...] = d_total[...].astype(BF16)
        y_out[...] = y_total[...].astype(BF16)


def feed_call(tokens, cots, near, far):
    count, features = tokens.shape
    quarter = near.shape[0] // 3
    block = quarter // UNIT_STEPS

    def part(index):
        return pl.BlockSpec((block, features), lambda i: (UNIT_STEPS * index + i, 0))

    whole = pl.BlockSpec((count, features), lambda i: (0, 0))
    unit_out = pl.BlockSpec((block, count), lambda i: (i, 0))
    outs = pl.pallas_call(
        feed_kernel,
        grid=(UNIT_STEPS,),
        in_specs=[whole, whole] + [part(index) for index in range(3)] * 2,
        out_specs=[unit_out] * 6 + [whole, whole],
        out_shape=[jax.ShapeDtypeStruct((quarter, count), BF16)] * 6
        + [jax.ShapeDtypeStruct((count, features), BF16)] * 2,
        scratch_shapes=[pltpu.VMEM((count, features), F32)] * 2,
    )(tokens, cots, near, near, near, far, far, far)
    return outs[:3], outs[3:6], outs[6], outs[7]


def unit_grad_kernel(
    gate_o, up_o, hid_o, gate_m, up_m, hid_m, tok_o, tok_m, cot_o, cot_m, keep_out, sent_out
):
    quarter = gate_o.shape[0]
    for index, (own, mate, x_own, x_mate) in enumerate(
        ((gate_o, gate_m, tok_o, tok_m), (up_o, up_m, tok_o, tok_m), (hid_o, hid_m, cot_o, cot_m))
    ):
        total = (times(own[...], x_own[...]) + times(mate[...], x_mate[...])).astype(BF16)
        rows = slice(index * quarter, (index + 1) * quarter)
        for p in range(8):
            target = sent_out if p % 2 else keep_out
            target[rows, p // 2 * CHUNK : (p // 2 + 1) * CHUNK] = total[:, p * CHUNK : (p + 1) * CHUNK]


def unit_grads(own, mate, tok_o, tok_m, cot_o, cot_m):
    if not small_dp():
        pre = [times(own[i], tok_o) + times(mate[i], tok_m) for i in range(2)]
        down = times(own[2], cot_o) + times(mate[2], cot_m)
        return [jnp.concatenate(pre + [down], axis=0).astype(BF16)]
    half = ((3 * own[0].shape[0], tok_o.shape[1] // 2), BF16)
    keep, sent = row_call(unit_grad_kernel, [half, half], *own, *mate, tok_o, tok_m, cot_o, cot_m)
    got = swap(sent, "dp", 1)
    return [
        (mine.astype(F32) + other.astype(F32)).astype(BF16)
        for mine, other in zip(jnp.split(keep, 4, axis=1), jnp.split(got, 4, axis=1))
    ]


def row_call(kernel, outs, *args):
    def space(arg):
        kind = pltpu.SMEM if arg.dtype == jnp.int32 else pltpu.VMEM
        return pl.BlockSpec(memory_space=kind)

    return pl.pallas_call(
        kernel,
        in_specs=[space(a) for a in args],
        out_specs=[pl.BlockSpec(memory_space=pltpu.VMEM)] * len(outs),
        out_shape=[jax.ShapeDtypeStruct(s, d) for s, d in outs],
    )(*args)


def swap(value, axis, mask):
    pairs = [(i, i ^ mask) for i in range(lax.axis_size(axis))]
    return lax.ppermute(value, axis, pairs)


def planar_swaps(blocks):
    moved = [blocks[0]]
    for q in range(1, 4):
        moved.append(swap(blocks[q], "dp", 2 * q))
    return moved


def small_dp():
    return lax.axis_size("dp") == 8


def planar_dp(own):
    if not small_dp():
        return [own]
    return planar_swaps([own] * 4)


def core_dp(across):
    return [swap(piece, "dp", 1) for piece in across] if small_dp() else []


def join_dp(across, beside, axis):
    if not small_dp():
        return lax.all_gather(across[0], "dp", axis=axis, tiled=True)
    return jnp.concatenate([piece for pair in zip(across, beside) for piece in pair], axis=axis)


def beside_dp(across, axis):
    return join_dp(across, core_dp(across), axis)


def core_sum(blocks, axis):
    sent = swap(jnp.concatenate(blocks[1::2], axis=axis), "dp", 1)
    return [
        (mine.astype(F32) + other.astype(F32)).astype(BF16)
        for mine, other in zip(blocks[0::2], jnp.split(sent, 4, axis=axis))
    ]


def core_half(partials):
    if not small_dp():
        return [jnp.concatenate(partials, axis=0)]
    split = [jnp.split(partial, 8, axis=1) for partial in partials]
    return core_sum([jnp.concatenate(group, axis=0) for group in zip(*split)], 1)


def core_rows_half(partial):
    return core_sum(jnp.split(partial, 8, axis=0), 0) if small_dp() else [partial]


def planar_move(half, axis):
    if not small_dp():
        return [lax.psum_scatter(half[0], "dp", scatter_dimension=axis, tiled=True)]
    return planar_swaps(half)


def planar_sum(half, axis):
    return sum(piece.astype(F32) for piece in planar_move(half, axis))


def tree_sum(value, axis):
    parts = [value] + [swap(value, axis, mask) for mask in range(1, lax.axis_size(axis))]
    while len(parts) > 1:
        parts = [left + right for left, right in zip(parts[0::2], parts[1::2])]
    return parts[0]


def after(value, anchor):
    return lax.optimization_barrier((value, anchor))[0]


def layer(
    inputs,
    segments,
    cotangent,
    norm_in,
    w_in,
    w_alpha_beta,
    conv_weight,
    a_log,
    dt_bias,
    out_gain,
    w_out,
    norm_ffn,
    w_gate,
    w_up,
    w_down,
):
    doc_ids = segments[0]
    length = doc_ids.shape[0]
    rows, features = inputs.shape
    part_index = lax.axis_index("tensor")
    parts = lax.axis_size("tensor")
    head_count = a_log.shape[0] // parts
    conv_width = head_count * CONVW
    hidden_units = w_down.shape[0]
    order = lax.axis_index("dp") if small_dp() else jnp.zeros((), jnp.int32)
    me = order.astype(jnp.int32)[None]
    conv_mine = lax.dynamic_slice_in_dim(conv_weight, part_index * conv_width, conv_width, 1)
    alog_mine = lax.dynamic_slice_in_dim(a_log, part_index * head_count, head_count, 0)
    bias_mine = lax.dynamic_slice_in_dim(dt_bias, part_index * head_count, head_count, 0)
    docs = jnp.broadcast_to(doc_ids.astype(F32)[:, None], (length, CHUNK))
    lane_pair = jnp.stack([jnp.exp(alog_mine), bias_mine])
    spread = jnp.stack([lane_pair, jnp.zeros_like(lane_pair)], axis=-1).reshape(2, 2 * head_count)
    vectors = jnp.pad(spread, ((0, 6), (0, CHUNK - 2 * head_count)))
    gain_row = out_gain[None, :]

    token_bf, token_f32 = ((rows, features), BF16), ((rows, features), F32)
    gain_shape = ((1, features), F32)
    x, cot, normed, gain_in, gain_ffn = row_call(
        prepare_kernel, [token_bf, token_bf, token_bf, gain_shape, gain_shape],
        me, inputs, cotangent, norm_in[None], norm_ffn[None],
    )
    joined = jnp.concatenate(
        [w_in, jnp.pad(w_alpha_beta, ((0, 0), (0, CHUNK - w_alpha_beta.shape[1])))], axis=1
    )
    units = jnp.concatenate([w_gate.T, w_up.T, w_down], axis=0)
    seq_rows = lax.all_gather(normed, "tensor", axis=0, tiled=True)
    joined, out_block = after((joined, w_out), normed)
    whole_in = beside_dp(planar_dp(joined), 0)
    whole_out = beside_dp(planar_dp(out_block), 1)
    near = planar_dp(after(units, (whole_in, whole_out)))
    far_units = swap(after(units, seq_rows), "tensor", 2)
    mate_cot = swap(after(cot, seq_rows), "tensor", 1)
    projected = times(seq_rows, whole_in)
    gated, *kept = mixer_forward(projected, docs, conv_mine, vectors, gain_row)
    mixed_part = times(gated, whole_out).astype(BF16)
    mixed = lax.psum_scatter(mixed_part, "tensor", scatter_dimension=0, tiled=True)
    far = planar_dp(after(far_units, gated))
    near = after(near, gated)
    weights = [beside_dp(near, 1), beside_dp(far, 1)]
    mixed, weights, mate_cot = lax.optimization_barrier((mixed, weights, mate_cot))
    resid, normed_ffn = row_call(middle_kernel, [token_f32, token_bf], x, mixed, gain_ffn)

    mate_normed = swap(normed_ffn, "tensor", 1)
    near_own, far_own, d_own, out_own = feed_call(normed_ffn, cot, *weights)
    near_mate, far_mate, d_mate, out_mate = feed_call(mate_normed, mate_cot, *weights)
    d_from_mate = swap(d_mate, "tensor", 1)
    activations_all = (normed_ffn, mate_normed, cot, mate_cot)
    far_half = unit_grads(after(far_own, d_mate), far_mate, *activations_all)
    near_half = unit_grads(after(near_own, far_half), near_mate, *activations_all)
    d_resid, d_mixed, gain_ffn_part = row_call(
        ffn_back_kernel, [token_f32, token_bf, gain_shape],
        me, resid, cot, d_own, d_from_mate, gain_ffn,
    )

    mixer_back_seq = lax.all_gather(d_mixed, "tensor", axis=0, tiled=True)
    far_grad = planar_sum(far_half, 1).astype(BF16)
    near_half, far_grad = lax.optimization_barrier((near_half, far_grad))
    out_mate = after(out_mate, mixer_back_seq)
    from_far = swap(far_grad, "tensor", 2)
    near_moved = planar_move(near_half, 1)
    out_from_mate = swap(out_mate, "tensor", 1)
    d_gated = times_transposed(mixer_back_seq, whole_out)
    d_projected, d_conv, d_vectors, d_gain_out = mixer_backward(
        projected, docs, conv_mine, vectors, gain_row, kept, d_gated
    )
    d_part = times_transposed(d_projected, whole_in).astype(BF16)
    d_normed_in = lax.psum_scatter(d_part, "tensor", scatter_dimension=0, tiled=True)
    seq_later, gated_later, back_later = after((seq_rows, gated, mixer_back_seq), d_part)
    joined_half = core_rows_half(transposed_times(seq_later, d_projected).astype(BF16))
    grad_joined = planar_sum(joined_half, 0)
    (gain_in_part,) = row_call(gain_kernel, [gain_shape], me, d_part, seq_later, gain_in)
    out_half = core_half([transposed_times(gated_later, back_later).astype(BF16)])
    grad_out = planar_sum(after(out_half, joined_half), 1)
    out_from_mate, near_moved, from_far = after((out_from_mate, near_moved, from_far), joined_half)
    (output,) = row_call(output_kernel, [token_bf], me, resid, out_own, out_from_mate)
    grad_units = sum(piece.astype(F32) for piece in near_moved) + from_far.astype(F32)
    (d_inputs,) = row_call(finish_kernel, [token_f32], me, x, d_resid, d_normed_in, gain_in)

    last = jnp.concatenate(
        [
            d_gain_out,
            d_vectors[:1, : 2 * head_count],
            d_vectors[1:2, : 2 * head_count],
        ],
        axis=1,
    )
    last = jnp.pad(last, ((0, 0), (0, conv_width - last.shape[1])))
    if conv_width == features:
        table = jnp.concatenate([d_conv, gain_in_part, gain_ffn_part, last], axis=0)
        table = after(table, joined_half)
        table = tree_sum(table, "dp") if small_dp() else lax.psum(table, "dp")
        tables = [table] + [swap(table, "tensor", mask) for mask in range(1, parts)]
    else:
        raise ValueError("conv width")
    shared = [t[4:] for t in tables]
    while len(shared) > 1:
        shared = [left + right for left, right in zip(shared[0::2], shared[1::2])]
    shared = shared[0]
    grad_conv = jnp.zeros(conv_weight.shape, F32)
    own_rows = jnp.zeros((2, a_log.shape[0]), F32)
    width = out_gain.shape[0]
    for mask, t in enumerate(tables):
        place_index = part_index ^ mask
        grad_conv = lax.dynamic_update_slice_in_dim(grad_conv, t[:4], place_index * conv_width, 1)
        pair = t[6, width : width + 4 * head_count].reshape(2, 2 * head_count)[:, ::2]
        own_rows = lax.dynamic_update_slice_in_dim(own_rows, pair, place_index * head_count, 1)
    columns = w_in.shape[1]
    return (
        output,
        d_inputs,
        shared[0],
        grad_joined[:, :columns],
        grad_joined[:, columns : columns + w_alpha_beta.shape[1]],
        grad_conv,
        own_rows[0],
        own_rows[1],
        shared[2, :width],
        grad_out,
        shared[1],
        grad_units[:hidden_units].T,
        grad_units[hidden_units : 2 * hidden_units].T,
        grad_units[2 * hidden_units :],
    )


def solution(mesh):
    return jax.shard_map(
        layer,
        mesh=mesh,
        in_specs=(
            P(("dp", "tensor"), None),
            P("dp", None),
            P(("dp", "tensor"), None),
            P(),
            P("dp", "tensor"),
            P("dp", "tensor"),
            P(),
            P(),
            P(),
            P(),
            P("tensor", "dp"),
            P(),
            P("dp", "tensor"),
            P("dp", "tensor"),
            P("tensor", "dp"),
        ),
        out_specs=(
            P(("dp", "tensor"), None),
            P(("dp", "tensor"), None),
            P(),
            P("dp", "tensor"),
            P("dp", "tensor"),
            P(),
            P(),
            P(),
            P(),
            P("tensor", "dp"),
            P(),
            P("dp", "tensor"),
            P("dp", "tensor"),
            P("tensor", "dp"),
        ),
        check_vma=False,
    )
```

```python
import functools
import math
import jax
import jax.numpy as jnp
from jax import lax
from jax.experimental import pallas as pl
from jax.experimental.pallas import tpu as pltpu

from jax.sharding import PartitionSpec as P

DK = 128
DV = 256
CONVW = 2 * DK + DV
HEADW = 2 * DK + 2 * DV
CHUNK = 128
SUBS = 2
EPSILON = 1e-06
F32 = jnp.float32
BF16 = jnp.bfloat16
NN = (((1,), (0,)), ((), ()))
NT = (((1,), (1,)), ((), ()))
TN = (((0,), (0,)), ((), ()))


def split(value):
    high = value.astype(BF16)
    return high, (value - high.astype(F32)).astype(BF16)


def dot3(left, right, dims=NN):
    lh, ll = left if isinstance(left, tuple) else split(left)
    rh, rl = right if isinstance(right, tuple) else split(right)
    (l_axis,), (r_axis,) = dims[0]
    return lax.dot_general(
        jnp.concatenate([lh, lh, ll], axis=l_axis),
        jnp.concatenate([rh, rl, rh], axis=r_axis),
        dims,
        preferred_element_type=F32,
    )


def sigmoid(x):
    return 1.0 / (1.0 + jnp.exp(-x))


def softplus(x):
    return jnp.maximum(x, 0.0) + jnp.log(1.0 + jnp.exp(-jnp.abs(x)))


def place(shape, axis):
    return lax.broadcasted_iota(jnp.int32, shape, axis)


def cumulate(value, backwards=False):
    length = value.shape[0]
    row = place(value.shape, 0)
    step = 1
    while step < length:
        if backwards:
            moved = pltpu.roll(value, length - step, 0)
            value = value + jnp.where(row < length - step, moved, 0.0)
        else:
            moved = pltpu.roll(value, step, 0)
            value = value + jnp.where(row >= step, moved, 0.0)
        step *= 2
    return value


def conv_parts(before, rows, doc_before, docs):
    length = rows.shape[0]
    tall = jnp.concatenate([before, rows], axis=0)
    tall_docs = jnp.concatenate([doc_before, docs], axis=0)
    parts = [rows]
    for offset in range(1, 4):
        same = tall_docs[8 - offset : 8 - offset + length, :1] == docs[:, :1]
        parts.append(jnp.where(same, tall[8 - offset : 8 - offset + length], 0.0))
    return parts


def head_decay(cum, lane, docs, doc_row, doc_carried):
    square = docs.shape
    g_col = jnp.broadcast_to(cum[:, lane : lane + 1], square)
    g_row = jnp.transpose(g_col)
    row, col = place(square, 0), place(square, 1)
    seen = (row >= col) & (docs == doc_row)
    fade = jnp.where(seen, jnp.exp(jnp.where(seen, g_col - g_row, 0.0)), 0.0)
    strict = jnp.where(row > col, fade, 0.0)
    reach = jnp.where(docs == doc_carried, jnp.exp(g_col), 0.0)
    g_last = g_col[-1:, :]
    doc_last = docs[-1:, :]
    trail = jnp.where(docs == doc_last, jnp.exp(g_last - g_col), 0.0)
    keep = jnp.where(doc_last == doc_carried, jnp.exp(g_last), 0.0)
    return fade, strict, reach, trail, keep


def unit_lower_inverses(lowers):
    square = lowers[0].shape
    row, col = place(square, 0), place(square, 1)
    apart = row ^ col
    inverses = [
        jnp.where(row == col, 1.0, jnp.where(apart == 1, -lower, 0.0)) for lower in lowers
    ]
    level = 1
    while (1 << level) < square[0]:
        across = (apart >> level) == 1
        pairs = [split(inverse) for inverse in inverses]
        inner = [
            dot3(jnp.where(across, lower, 0.0), pair) for lower, pair in zip(lowers, pairs)
        ]
        inverses = [
            inverse - dot3(pair, part) for inverse, pair, part in zip(inverses, pairs, inner)
        ]
        level += 1
    return inverses


def activations(proj_ref, before_ref, conv_ref, docs, doc_before, head):
    base = head * HEADW
    rows = proj_ref[:, base : base + CONVW]
    before = before_ref[:, base : base + CONVW]
    taps = conv_ref[:, head * CONVW : (head + 1) * CONVW]
    parts = conv_parts(before, rows, doc_before, docs)
    pre = sum(parts[s] * taps[s : s + 1] for s in range(4))
    gate = sigmoid(pre)
    post = pre * gate
    q_raw, k_raw, value = post[:, :DK], post[:, DK : 2 * DK], post[:, 2 * DK :]
    q_scale = lax.rsqrt(jnp.sum(q_raw * q_raw, axis=-1, keepdims=True) + EPSILON)
    k_scale = lax.rsqrt(jnp.sum(k_raw * k_raw, axis=-1, keepdims=True) + EPSILON)
    query = q_raw * q_scale * DK ** (-0.5)
    key = k_raw * k_scale
    return parts, taps, pre, gate, q_raw, k_raw, q_scale, k_scale, query, key, value


def doc_context(doc_ref, doc_before_ref, chunk):
    docs = doc_ref[...]
    doc_before = jnp.where(chunk > 0, doc_before_ref[...], -1.0)
    doc_row = jnp.transpose(docs) if docs.shape[0] == CHUNK else None
    return docs, doc_row, doc_before, doc_before[-1:, :]


def forward_kernel(
    heads, seq_ref, weight_ref, doc_ref, doc_before_ref, conv_ref, vec_ref, gain_ref,
    proj_ref, gated_ref, recur_ref, inverse_ref, solved_ref, mix_ref, key_ref, tilde_ref, start_ref, state, before_ref,
):
    step = pl.program_id(0)

    @pl.when(step == 0)
    def _():
        state[...] = jnp.zeros_like(state)
        before_ref[...] = jnp.zeros_like(before_ref)

    proj_ref[...] = lax.dot_general(
        seq_ref[...], weight_ref[...], NN, preferred_element_type=F32
    )
    docs_all, _, doc_before, doc_carried = doc_context(doc_ref, doc_before_ref, step)
    pair = proj_ref[:, heads * HEADW :]
    decay = -vec_ref[0:1, :] * softplus(pair + vec_ref[1:2, :])
    write = sigmoid(pair)
    acts = [
        activations(proj_ref, before_ref, conv_ref, docs_all, doc_before, head)[8:]
        for head in range(heads)
    ]
    units = []
    for sub in range(docs_all.shape[0] // CHUNK):
        rows = slice(sub * CHUNK, (sub + 1) * CHUNK)
        docs = docs_all[rows]
        doc_row = jnp.transpose(docs)
        carried = doc_carried if sub == 0 else docs_all[sub * CHUNK - 1 : sub * CHUNK]
        cum = cumulate(decay[rows])
        for head in range(heads):
            query, key, value = [part[rows] for part in acts[head]]
            decays = head_decay(cum, 2 * head, docs, doc_row, carried)
            beta = write[rows, 2 * head + 1 : 2 * head + 2]
            units.append((sub, head, rows, query, key, value, beta, decays))
    lowers, mixes = [], []
    for sub, head, rows, query, key, value, beta, decays in units:
        both = dot3(jnp.concatenate([key, query], axis=0), split(key), NT)
        key_key = both[:CHUNK] * decays[1]
        key_ref[sub, head] = key_key
        lowers.append(beta * key_key)
        mixes.append(both[CHUNK:] * decays[0])
    inverses = unit_lower_inverses(lowers)
    eye = place((CHUNK, CHUNK), 0) == place((CHUNK, CHUNK), 1)
    ready = []
    for unit, inverse, mix in zip(units, inverses, mixes):
        sub, head, rows, query, key, value, beta, (fade, strict, reach, trail, keep) = unit
        rhs = jnp.concatenate([beta * reach * key, beta * value], axis=1)
        solved = dot3(inverse, rhs)
        trailing = jnp.transpose(trail * key)
        outer = dot3(jnp.concatenate([trailing, mix], axis=0), solved)
        step_matrix = jnp.where(eye, keep, 0.0) - outer[:CHUNK, :DK]
        tilde = jnp.concatenate([step_matrix, reach * query - outer[CHUNK:, :DK]], axis=0)
        inverse_ref[sub, head] = inverse
        solved_ref[sub, head] = solved
        mix_ref[sub, head] = mix
        tilde_ref[sub, head] = tilde
        ready.append((sub, head, rows, tilde, outer))
    for sub, head, rows, tilde, outer in ready:
        start = state[head]
        start_ref[sub, head] = start
        moved = dot3(tilde, start)
        state[head] = moved[:CHUNK] + outer[:CHUNK, DK:]
        recurrent = moved[CHUNK:] + outer[CHUNK:, DK:]
        recur_ref[rows, head * DV : (head + 1) * DV] = recurrent
        scale = lax.rsqrt(jnp.mean(recurrent * recurrent, axis=-1, keepdims=True) + EPSILON)
        z = proj_ref[rows, head * HEADW + CONVW : (head + 1) * HEADW]
        gated = recurrent * scale * gain_ref[...] * (z * sigmoid(z))
        gated_ref[rows, head * DV : (head + 1) * DV] = gated.astype(BF16)
    before_ref[...] = proj_ref[proj_ref.shape[0] - 8 :, :]


def backward_kernel(
    heads, chunks, proj_ref, before_ref, doc_ref, doc_before_ref, doc_after_ref,
    conv_ref, vec_ref, gain_ref, recur_ref, inverse_ref, solved_ref, mix_ref, key_ref, tilde_ref,
    start_ref, back_ref, out_weight_ref,
    d_proj_ref, d_conv_ref, d_vec_ref, d_gain_ref, d_state, d_after,
):
    step_index = pl.program_id(0)
    chunk = chunks - 1 - step_index

    @pl.when(step_index == 0)
    def _():
        d_state[...] = jnp.zeros_like(d_state)
        d_after[...] = jnp.zeros_like(d_after)
        d_conv_ref[...] = jnp.zeros_like(d_conv_ref)
        d_vec_ref[...] = jnp.zeros_like(d_vec_ref)
        d_gain_ref[...] = jnp.zeros_like(d_gain_ref)

    docs, doc_row, doc_before, doc_carried = doc_context(doc_ref, doc_before_ref, chunk)
    tall_docs = jnp.concatenate([docs, doc_after_ref[...]], axis=0)
    pair = proj_ref[:, heads * HEADW :]
    shifted = pair + vec_ref[1:2, :]
    decay = -vec_ref[0:1, :] * softplus(shifted)
    write = sigmoid(pair)
    cum = cumulate(decay)
    lanes = place(docs.shape, 1)
    last_row = place(docs.shape, 0) == CHUNK - 1
    d_cum = jnp.zeros_like(docs)
    d_write = jnp.zeros_like(docs)
    grad_all = lax.dot_general(
        back_ref[...], out_weight_ref[...], NT, preferred_element_type=F32
    )
    for head in range(heads):
        acts = activations(proj_ref, before_ref, conv_ref, docs, doc_before, head)
        parts, taps, pre, gate, q_raw, k_raw, q_scale, k_scale, query, key, value = acts
        fade, strict, reach, trail, keep = head_decay(cum, 2 * head, docs, doc_row, doc_carried)
        beta = write[:, 2 * head + 1 : 2 * head + 2]
        grad = grad_all[:, head * DV : (head + 1) * DV]
        recurrent = recur_ref[:, head * DV : (head + 1) * DV]
        scale = lax.rsqrt(jnp.mean(recurrent * recurrent, axis=-1, keepdims=True) + EPSILON)
        z = proj_ref[:, head * HEADW + CONVW : (head + 1) * HEADW]
        z_gate = sigmoid(z)
        unit = recurrent * scale
        gain = gain_ref[...]
        d_normed = grad * (z * z_gate)
        d_z = grad * unit * gain * (z_gate * (1.0 + z * (1.0 - z_gate)))
        d_gain_ref[...] += jnp.sum(d_normed * unit, axis=0, keepdims=True)
        weighted = d_normed * gain
        d_out = scale * (weighted - unit * jnp.mean(weighted * unit, axis=-1, keepdims=True))
        inverse = inverse_ref[0, head]
        solved = solved_ref[0, head]
        mix = mix_ref[0, head]
        key_key = key_ref[0, head]
        tilde = tilde_ref[0, head]
        start = start_ref[0, head]
        d_next = d_state[head]
        flow = jnp.concatenate([d_next, d_out], axis=0)
        d_state[head] = dot3(tilde, flow, TN)
        start_pair = split(start)
        delta = solved[:, DK:] - dot3(solved[:, :DK], start_pair)
        trailing = trail * key
        d_delta = dot3(jnp.concatenate([trailing, jnp.transpose(mix)], axis=1), flow)
        d_rhs = dot3(inverse, d_delta, TN)
        grads = jnp.concatenate([d_out, d_rhs], axis=0)
        outer = dot3(grads, delta, NT)
        onto = dot3(grads, start_pair, NT)
        d_mix = outer[:CHUNK]
        d_lower = -outer[CHUNK:]
        from_next = dot3(delta, d_next, NT)
        mixed = d_mix * fade
        lowered = d_lower * strict * beta
        d_query = reach * onto[:CHUNK] + dot3(mixed, key)
        d_key = (
            dot3(jnp.transpose(mixed), query)
            + dot3(lowered + jnp.transpose(lowered), key)
            + trail * from_next
            - beta * reach * onto[CHUNK:]
        )
        d_value = beta * d_rhs
        crossed = d_lower * key_key
        net = d_mix * mix + beta * crossed
        reach_col = reach[:, :1]
        sum_query = jnp.sum(query * onto[:CHUNK], axis=-1, keepdims=True)
        sum_key = jnp.sum(key * onto[CHUNK:], axis=-1, keepdims=True)
        sum_trail = jnp.sum(trailing * from_next, axis=-1, keepdims=True)
        d_beta = (
            jnp.sum(crossed, axis=-1, keepdims=True)
            + jnp.sum(d_rhs * value, axis=-1, keepdims=True)
            - reach_col * sum_key
        )
        d_g = (
            jnp.sum(net - jnp.transpose(net), axis=-1, keepdims=True)
            + reach_col * sum_query
            - beta * reach_col * sum_key
            - sum_trail
        )
        kept = keep[:, :1] * jnp.sum(
            jnp.sum(start * d_next, axis=-1, keepdims=True), axis=0, keepdims=True
        )
        d_last = jnp.sum(sum_trail, axis=0, keepdims=True) + kept
        d_g = d_g + jnp.where(last_row[:, :1], d_last, 0.0)
        d_cum = jnp.where(lanes == 2 * head, d_g, d_cum)
        d_write = jnp.where(lanes == 2 * head + 1, d_beta, d_write)
        d_q_raw = (
            (d_query - q_raw * (q_scale * q_scale) * jnp.sum(d_query * q_raw, axis=-1, keepdims=True))
            * q_scale * DK ** (-0.5)
        )
        d_k_raw = (
            d_key - k_raw * (k_scale * k_scale) * jnp.sum(d_key * k_raw, axis=-1, keepdims=True)
        ) * k_scale
        d_post = jnp.concatenate([d_q_raw, d_k_raw, d_value], axis=1)
        d_pre = d_post * gate * (1.0 + pre * (1.0 - gate))
        columns = slice(head * CONVW, (head + 1) * CONVW)
        d_conv_ref[:, columns] += jnp.concatenate(
            [jnp.sum(d_pre * parts[s], axis=0, keepdims=True) for s in range(4)], axis=0
        )
        tall = jnp.concatenate([d_pre, d_after[:, columns]], axis=0)
        d_rows = d_pre * taps[0:1]
        for offset in range(1, 4):
            same = tall_docs[offset : offset + CHUNK, :1] == docs[:, :1]
            d_rows = d_rows + jnp.where(
                same, tall[offset : offset + CHUNK] * taps[offset : offset + 1], 0.0
            )
        d_after[:, columns] = d_pre[:8]
        d_proj_ref[:, head * HEADW : head * HEADW + CONVW] = d_rows.astype(BF16)
        d_proj_ref[:, head * HEADW + CONVW : (head + 1) * HEADW] = d_z.astype(BF16)
    d_decay = cumulate(d_cum, backwards=True)
    d_shifted = d_decay * -vec_ref[0:1, :] * sigmoid(shifted)
    d_written = d_write * write * (1.0 - write)
    used = lanes < 2 * heads
    even = (lanes & 1) == 0
    d_proj_ref[:, heads * HEADW :] = jnp.where(used, jnp.where(even, d_shifted, d_written), 0.0).astype(BF16)
    d_vec_ref[0:1, :] += jnp.sum(d_decay * decay, axis=0, keepdims=True)
    d_vec_ref[1:2, :] += jnp.sum(d_shifted, axis=0, keepdims=True)


def chunk_specs(heads, chunks, where, subs=1):
    size = subs * CHUNK
    per8 = size // 8

    def rows(width):
        return pl.BlockSpec((size, width), lambda c: (where(c), 0))

    def before(width):
        return pl.BlockSpec((8, width), lambda c: (jnp.maximum(where(c) * per8 - 1, 0), 0))

    def after(width):
        return pl.BlockSpec(
            (8, width), lambda c: (jnp.minimum((where(c) + 1) * per8, chunks * per8 - 1), 0)
        )

    def whole(shape):
        return pl.BlockSpec(shape, lambda c: (0,) * len(shape))

    def saved(height, width):
        return pl.BlockSpec((subs, heads, height, width), lambda c: (where(c), 0, 0, 0))

    return rows, before, after, whole, saved


def saved_shapes():
    sizes = ((CHUNK, CHUNK), (CHUNK, DK + DV), (CHUNK, CHUNK), (CHUNK, CHUNK), (2 * CHUNK, DK), (DK, DV))
    return sizes


def mixer_forward(seq_rows, weight, docs, taps, vectors, gain, interpret=False):
    length, features = seq_rows.shape
    width = weight.shape[1]
    heads = (width - CHUNK) // HEADW
    chunks = length // CHUNK
    subs = math.gcd(chunks, SUBS)
    rows, before, _, whole, saved = chunk_specs(heads, chunks, lambda c: c, subs)
    sizes = saved_shapes()
    return pl.pallas_call(
        functools.partial(forward_kernel, heads),
        grid=(chunks // subs,),
        in_specs=[
            rows(features), whole((features, width)), rows(CHUNK), before(CHUNK),
            whole((4, heads * CONVW)), whole((8, CHUNK)), whole((1, DV)),
        ],
        out_specs=[rows(width), rows(heads * DV), rows(heads * DV)] + [saved(*s) for s in sizes],
        out_shape=[
            jax.ShapeDtypeStruct((length, width), F32),
            jax.ShapeDtypeStruct((length, heads * DV), BF16),
            jax.ShapeDtypeStruct((length, heads * DV), F32),
        ]
        + [jax.ShapeDtypeStruct((chunks, heads) + s, F32) for s in sizes],
        scratch_shapes=[pltpu.VMEM((heads, DK, DV), F32), pltpu.VMEM((8, width), F32)],
        name="mixer_forward",
        interpret=interpret,
    )(seq_rows, weight, docs, docs, taps, vectors, gain)


def mixer_backward(
    projected, docs, taps, vectors, gain, kept, back_seq, out_weight, interpret=False
):
    length, width = projected.shape
    features = back_seq.shape[1]
    heads = (width - CHUNK) // HEADW
    chunks = length // CHUNK
    rows, before, after, whole, saved = chunk_specs(heads, chunks, lambda c: chunks - 1 - c)
    sizes = saved_shapes()
    return pl.pallas_call(
        functools.partial(backward_kernel, heads, chunks),
        grid=(chunks,),
        in_specs=[
            rows(width), before(width), rows(CHUNK), before(CHUNK), after(CHUNK),
            whole((4, heads * CONVW)), whole((8, CHUNK)), whole((1, DV)), rows(heads * DV),
        ]
        + [saved(*s) for s in sizes]
        + [rows(features), whole((heads * DV, features))],
        out_specs=[
            rows(width), whole((4, heads * CONVW)), whole((8, CHUNK)), whole((1, DV)),
        ],
        out_shape=[
            jax.ShapeDtypeStruct((length, width), BF16),
            jax.ShapeDtypeStruct((4, heads * CONVW), F32),
            jax.ShapeDtypeStruct((8, CHUNK), F32),
            jax.ShapeDtypeStruct((1, DV), F32),
        ],
        scratch_shapes=[pltpu.VMEM((heads, DK, DV), F32), pltpu.VMEM((8, heads * CONVW), F32)],
        name="mixer_backward",
        interpret=interpret,
    )(projected, projected, docs, docs, docs, taps, vectors, gain, *kept, back_seq, out_weight)


def times_transposed(left, right):
    return lax.dot_general(left, right, NT, preferred_element_type=F32)


def transposed_times(left, right):
    return lax.dot_general(left, right, TN, preferred_element_type=F32)


def times(left, right):
    return lax.dot_general(left, right, NN, preferred_element_type=F32)


def block_source(me_ref, place_index, width):
    return pl.ds(pl.multiple_of((me_ref[0] ^ place_index) * width, width), width)


def row_scale(values):
    return lax.rsqrt(jnp.mean(values * values, axis=-1, keepdims=True) + EPSILON)


def prepare_kernel(
    me_ref, x_ref, cot_ref, gain_in_ref, gain_ffn_ref,
    x_out, cot_out, normed_out, gain_in_out, gain_ffn_out,
):
    scale = row_scale(x_ref[...].astype(F32))
    for p in range(x_ref.shape[1] // CHUNK):
        here, source = pl.ds(p * CHUNK, CHUNK), block_source(me_ref, p, CHUNK)
        part = x_ref[:, source]
        gain = gain_in_ref[:, source]
        x_out[:, here] = part
        cot_out[:, here] = cot_ref[:, source]
        normed_out[:, here] = (part.astype(F32) * scale * gain).astype(BF16)
        gain_in_out[:, here] = gain
        gain_ffn_out[:, here] = gain_ffn_ref[:, source]


def middle_kernel(x_ref, mixed_ref, gain_ref, resid_out, normed_out):
    resid = x_ref[...].astype(F32) + mixed_ref[...].astype(F32)
    resid_out[...] = resid
    normed_out[...] = (resid * row_scale(resid) * gain_ref[...]).astype(BF16)


def ffn_back_kernel(me_ref, resid_ref, cot_ref, grad_ref, mate_ref, gain_ref, d_resid_out, d_mixed_out, d_gain_out):
    resid = resid_ref[...]
    grad = grad_ref[...].astype(F32) + mate_ref[...].astype(F32)
    scale = row_scale(resid)
    unit = resid * scale
    weighted = grad * gain_ref[...]
    inner = jnp.mean(weighted * unit, axis=-1, keepdims=True)
    d_resid = cot_ref[...].astype(F32) + scale * (weighted - unit * inner)
    d_resid_out[...] = d_resid
    d_mixed_out[...] = d_resid.astype(BF16)
    sums = jnp.sum(grad * unit, axis=0, keepdims=True)
    for p in range(resid.shape[1] // CHUNK):
        d_gain_out[:, block_source(me_ref, p, CHUNK)] = sums[:, p * CHUNK : (p + 1) * CHUNK]


def output_kernel(me_ref, resid_ref, own_ref, mate_ref, out_ref):
    for p in range(resid_ref.shape[1] // CHUNK):
        here = pl.ds(p * CHUNK, CHUNK)
        ffn = own_ref[:, here].astype(F32) + mate_ref[:, here].astype(F32)
        total = resid_ref[:, here] + ffn
        out_ref[:, block_source(me_ref, p, CHUNK)] = total.astype(BF16)


def gain_kernel(me_ref, grad_ref, normed_ref, gain_ref, out_ref):
    sums = jnp.sum(grad_ref[...].astype(F32) * normed_ref[...].astype(F32), axis=0, keepdims=True)
    sums = sums / gain_ref[...]
    for p in range(grad_ref.shape[1] // CHUNK):
        out_ref[:, block_source(me_ref, p, CHUNK)] = sums[:, p * CHUNK : (p + 1) * CHUNK]


def finish_kernel(me_ref, x_ref, d_resid_ref, grad_ref, gain_ref, out_ref):
    x = x_ref[...].astype(F32)
    scale = row_scale(x)
    unit = x * scale
    weighted = grad_ref[...].astype(F32) * gain_ref[...]
    inner = jnp.mean(weighted * unit, axis=-1, keepdims=True)
    total = d_resid_ref[...] + scale * (weighted - unit * inner)
    for p in range(x.shape[1] // CHUNK):
        out_ref[:, block_source(me_ref, p, CHUNK)] = total[:, p * CHUNK : (p + 1) * CHUNK]


def feed_kernel(tok_ref, cot_ref, near_ref, far_ref, *refs):
    outs, (d_out, y_out) = refs[:6], refs[6:8]
    quarter = near_ref.shape[0] // 3
    tokens, cots = tok_ref[...], cot_ref[...]
    d_total = y_total = 0.0
    for source, weights in enumerate((near_ref, far_ref)):
        gate_w, up_w, down_w = [
            weights.at[pl.ds(index * quarter, quarter)] for index in range(3)
        ]
        gate_pre = times_transposed(gate_w[...], tokens)
        up_pre = times_transposed(up_w[...], tokens)
        d_hidden = times_transposed(down_w[...], cots)
        sig = sigmoid(gate_pre)
        silu = gate_pre * sig
        hidden = (silu * up_pre).astype(BF16)
        d_up = (d_hidden * silu).astype(BF16)
        d_gate = (d_hidden * up_pre * (sig * (1.0 + gate_pre * (1.0 - sig)))).astype(BF16)
        for ref, value in zip(outs[3 * source : 3 * source + 3], (d_gate, d_up, hidden)):
            ref[...] = value
        d_total += transposed_times(d_gate, gate_w[...]) + transposed_times(d_up, up_w[...])
        y_total += transposed_times(hidden, down_w[...])
    d_out[...] = d_total.astype(BF16)
    y_out[...] = y_total.astype(BF16)


def feed_call(tokens, cots, near, far):
    count, features = tokens.shape
    quarter = near.shape[0] // 3
    in_vmem = pl.BlockSpec(memory_space=pltpu.VMEM)
    outs = pl.pallas_call(
        feed_kernel,
        in_specs=[in_vmem] * 4,
        out_specs=[in_vmem] * 8,
        out_shape=[jax.ShapeDtypeStruct((quarter, count), BF16)] * 6
        + [jax.ShapeDtypeStruct((count, features), BF16)] * 2,
    )(tokens, cots, near, far)
    return outs[:3], outs[3:6], outs[6], outs[7]


def unit_grad_kernel(
    gate_o, up_o, hid_o, gate_m, up_m, hid_m, tok_o, tok_m, cot_o, cot_m, keep_out, sent_out
):
    quarter = gate_o.shape[0]
    for index, (own, mate, x_own, x_mate) in enumerate(
        ((gate_o, gate_m, tok_o, tok_m), (up_o, up_m, tok_o, tok_m), (hid_o, hid_m, cot_o, cot_m))
    ):
        total = (times(own[...], x_own[...]) + times(mate[...], x_mate[...])).astype(BF16)
        rows = slice(index * quarter, (index + 1) * quarter)
        for p in range(8):
            target = sent_out if p % 2 else keep_out
            target[rows, p // 2 * CHUNK : (p // 2 + 1) * CHUNK] = total[:, p * CHUNK : (p + 1) * CHUNK]


def unit_grads(own, mate, tok_o, tok_m, cot_o, cot_m):
    if not small_dp():
        pre = [times(own[i], tok_o) + times(mate[i], tok_m) for i in range(2)]
        down = times(own[2], cot_o) + times(mate[2], cot_m)
        return [jnp.concatenate(pre + [down], axis=0).astype(BF16)]
    half = ((3 * own[0].shape[0], tok_o.shape[1] // 2), BF16)
    keep, sent = row_call(unit_grad_kernel, [half, half], *own, *mate, tok_o, tok_m, cot_o, cot_m)
    got = swap(sent, "dp", 1)
    return [
        (mine.astype(F32) + other.astype(F32)).astype(BF16)
        for mine, other in zip(jnp.split(keep, 4, axis=1), jnp.split(got, 4, axis=1))
    ]


def row_call(kernel, outs, *args):
    def space(arg):
        kind = pltpu.SMEM if arg.dtype == jnp.int32 else pltpu.VMEM
        return pl.BlockSpec(memory_space=kind)

    return pl.pallas_call(
        kernel,
        in_specs=[space(a) for a in args],
        out_specs=[pl.BlockSpec(memory_space=pltpu.VMEM)] * len(outs),
        out_shape=[jax.ShapeDtypeStruct(s, d) for s, d in outs],
    )(*args)


def swap(value, axis, mask):
    pairs = [(i, i ^ mask) for i in range(lax.axis_size(axis))]
    return lax.ppermute(value, axis, pairs)


def planar_swaps(blocks):
    moved = [blocks[0]]
    for q in range(1, 4):
        moved.append(swap(blocks[q], "dp", 2 * q))
    return moved


def small_dp():
    return lax.axis_size("dp") == 8


def planar_dp(own):
    if not small_dp():
        return [own]
    return planar_swaps([own] * 4)


def core_dp(across):
    return [swap(piece, "dp", 1) for piece in across] if small_dp() else []


def join_dp(across, beside, axis):
    if not small_dp():
        return lax.all_gather(across[0], "dp", axis=axis, tiled=True)
    return jnp.concatenate([piece for pair in zip(across, beside) for piece in pair], axis=axis)


def beside_dp(across, axis):
    return join_dp(across, core_dp(across), axis)


def core_sum(blocks, axis):
    sent = swap(jnp.concatenate(blocks[1::2], axis=axis), "dp", 1)
    return [
        (mine.astype(F32) + other.astype(F32)).astype(BF16)
        for mine, other in zip(blocks[0::2], jnp.split(sent, 4, axis=axis))
    ]


def core_half(partials):
    if not small_dp():
        return [jnp.concatenate(partials, axis=0)]
    split = [jnp.split(partial, 8, axis=1) for partial in partials]
    return core_sum([jnp.concatenate(group, axis=0) for group in zip(*split)], 1)


def core_rows_half(partial):
    return core_sum(jnp.split(partial, 8, axis=0), 0) if small_dp() else [partial]


def planar_move(half, axis):
    if not small_dp():
        return [lax.psum_scatter(half[0], "dp", scatter_dimension=axis, tiled=True)]
    return planar_swaps(half)


def planar_sum(half, axis):
    return sum(piece.astype(F32) for piece in planar_move(half, axis))


def turned(value, axis):
    parts = [value]
    for mask in range(1, lax.axis_size(axis)):
        parts.append(swap(value, axis, mask))
    return parts


def tree_sum(parts):
    while len(parts) > 1:
        parts = [left + right for left, right in zip(parts[0::2], parts[1::2])]
    return parts[0]


def after(value, anchor):
    return lax.optimization_barrier((value, anchor))[0]


def layer(
    inputs,
    segments,
    cotangent,
    norm_in,
    w_in,
    w_alpha_beta,
    conv_weight,
    a_log,
    dt_bias,
    out_gain,
    w_out,
    norm_ffn,
    w_gate,
    w_up,
    w_down,
):
    doc_ids = segments[0]
    length = doc_ids.shape[0]
    rows, features = inputs.shape
    part_index = lax.axis_index("tensor")
    parts = lax.axis_size("tensor")
    head_count = a_log.shape[0] // parts
    conv_width = head_count * CONVW
    hidden_units = w_down.shape[0]
    order = lax.axis_index("dp") if small_dp() else jnp.zeros((), jnp.int32)
    me = order.astype(jnp.int32)[None]
    conv_mine = lax.dynamic_slice_in_dim(conv_weight, part_index * conv_width, conv_width, 1)
    alog_mine = lax.dynamic_slice_in_dim(a_log, part_index * head_count, head_count, 0)
    bias_mine = lax.dynamic_slice_in_dim(dt_bias, part_index * head_count, head_count, 0)
    docs = jnp.broadcast_to(doc_ids.astype(F32)[:, None], (length, CHUNK))
    lane_pair = jnp.stack([jnp.exp(alog_mine), bias_mine])
    spread = jnp.stack([lane_pair, jnp.zeros_like(lane_pair)], axis=-1).reshape(2, 2 * head_count)
    vectors = jnp.pad(spread, ((0, 6), (0, CHUNK - 2 * head_count)))
    gain_row = out_gain[None, :]

    token_bf, token_f32 = ((rows, features), BF16), ((rows, features), F32)
    gain_shape = ((1, features), F32)
    x, cot, normed, gain_in, gain_ffn = row_call(
        prepare_kernel, [token_bf, token_bf, token_bf, gain_shape, gain_shape],
        me, inputs, cotangent, norm_in[None], norm_ffn[None],
    )
    joined = jnp.concatenate(
        [w_in, jnp.pad(w_alpha_beta, ((0, 0), (0, CHUNK - w_alpha_beta.shape[1])))], axis=1
    )
    units = jnp.concatenate([w_gate.T, w_up.T, w_down], axis=0)
    seq_rows = lax.all_gather(normed, "tensor", axis=0, tiled=True)
    joined, out_block = after((joined, w_out), normed)
    whole_in = beside_dp(planar_dp(joined), 0)
    whole_out = beside_dp(planar_dp(out_block), 1)
    near = planar_dp(after(units, (whole_in, whole_out)))
    far_units = swap(after(units, seq_rows), "tensor", 2)
    mate_cot = swap(after(cot, seq_rows), "tensor", 1)
    projected, gated, *kept = mixer_forward(seq_rows, whole_in, docs, conv_mine, vectors, gain_row)
    mixed_part = times(gated, whole_out).astype(BF16)
    mixed = lax.psum_scatter(mixed_part, "tensor", scatter_dimension=0, tiled=True)
    far = planar_dp(after(far_units, gated))
    near = after(near, gated)
    weights = [beside_dp(near, 1), beside_dp(far, 1)]
    mixed, weights, mate_cot = lax.optimization_barrier((mixed, weights, mate_cot))
    resid, normed_ffn = row_call(middle_kernel, [token_f32, token_bf], x, mixed, gain_ffn)

    mate_normed = swap(normed_ffn, "tensor", 1)
    near_own, far_own, d_own, out_own = feed_call(normed_ffn, cot, *weights)
    near_mate, far_mate, d_mate, out_mate = feed_call(mate_normed, mate_cot, *weights)
    d_from_mate = swap(d_mate, "tensor", 1)
    activations_all = (normed_ffn, mate_normed, cot, mate_cot)
    far_half = unit_grads(after(far_own, d_mate), far_mate, *activations_all)
    near_half = unit_grads(after(near_own, far_half[-1]), near_mate, *activations_all)
    d_resid, d_mixed, gain_ffn_part = row_call(
        ffn_back_kernel, [token_f32, token_bf, gain_shape],
        me, resid, cot, d_own, d_from_mate, gain_ffn,
    )

    mixer_back_seq = lax.all_gather(d_mixed, "tensor", axis=0, tiled=True)
    far_grad = planar_sum(far_half, 1).astype(BF16)
    near_half, far_grad = lax.optimization_barrier((near_half, far_grad))
    out_mate = after(out_mate, mixer_back_seq)
    from_far = swap(far_grad, "tensor", 2)
    near_moved = planar_move(near_half, 1)
    out_from_mate = swap(out_mate, "tensor", 1)
    d_projected, d_conv, d_vectors, d_gain_out = mixer_backward(
        projected, docs, conv_mine, vectors, gain_row, kept, mixer_back_seq, whole_out
    )
    d_part = times_transposed(d_projected, whole_in).astype(BF16)
    d_normed_in = lax.psum_scatter(d_part, "tensor", scatter_dimension=0, tiled=True)
    seq_later, gated_later, back_later = after((seq_rows, gated, mixer_back_seq), d_part)
    joined_half = core_rows_half(transposed_times(seq_later, d_projected).astype(BF16))
    grad_joined = planar_sum(joined_half, 0)
    (gain_in_part,) = row_call(gain_kernel, [gain_shape], me, d_part, seq_later, gain_in)
    out_half = core_half([transposed_times(gated_later, back_later).astype(BF16)])
    grad_out = planar_sum(after(out_half, joined_half[-1]), 1)
    out_from_mate, near_moved, from_far = after((out_from_mate, near_moved, from_far), joined_half[-1])
    (output,) = row_call(output_kernel, [token_bf], me, resid, out_own, out_from_mate)
    grad_units = sum(piece.astype(F32) for piece in near_moved) + from_far.astype(F32)
    (d_inputs,) = row_call(finish_kernel, [token_f32], me, x, d_resid, d_normed_in, gain_in)

    last = jnp.concatenate(
        [
            d_gain_out,
            d_vectors[:1, : 2 * head_count],
            d_vectors[1:2, : 2 * head_count],
        ],
        axis=1,
    )
    last = jnp.pad(last, ((0, 0), (0, conv_width - last.shape[1])))
    if conv_width == features:
        table = jnp.concatenate([d_conv, gain_in_part, gain_ffn_part, last], axis=0)
        table = after(table, joined_half[-1])
        if small_dp():
            table = turned(table, "dp")
            table = tree_sum(table)
        else:
            table = lax.psum(table, "dp")
        tables = turned(table, "tensor")
    else:
        raise ValueError("conv width")
    shared = tree_sum([t[4:] for t in tables])
    grad_conv = jnp.zeros(conv_weight.shape, F32)
    own_rows = jnp.zeros((2, a_log.shape[0]), F32)
    width = out_gain.shape[0]
    for mask, t in enumerate(tables):
        place_index = part_index ^ mask
        grad_conv = lax.dynamic_update_slice_in_dim(grad_conv, t[:4], place_index * conv_width, 1)
        pair = t[6, width : width + 4 * head_count].reshape(2, 2 * head_count)[:, ::2]
        own_rows = lax.dynamic_update_slice_in_dim(own_rows, pair, place_index * head_count, 1)
    columns = w_in.shape[1]
    return (
        output,
        d_inputs,
        shared[0],
        grad_joined[:, :columns],
        grad_joined[:, columns : columns + w_alpha_beta.shape[1]],
        grad_conv,
        own_rows[0],
        own_rows[1],
        shared[2, :width],
        grad_out,
        shared[1],
        grad_units[:hidden_units].T,
        grad_units[hidden_units : 2 * hidden_units].T,
        grad_units[2 * hidden_units :],
    )


def solution(mesh):
    return jax.shard_map(
        layer,
        mesh=mesh,
        in_specs=(
            P(("dp", "tensor"), None),
            P("dp", None),
            P(("dp", "tensor"), None),
            P(),
            P("dp", "tensor"),
            P("dp", "tensor"),
            P(),
            P(),
            P(),
            P(),
            P("tensor", "dp"),
            P(),
            P("dp", "tensor"),
            P("dp", "tensor"),
            P("tensor", "dp"),
        ),
        out_specs=(
            P(("dp", "tensor"), None),
            P(("dp", "tensor"), None),
            P(),
            P("dp", "tensor"),
            P("dp", "tensor"),
            P(),
            P(),
            P(),
            P(),
            P("tensor", "dp"),
            P(),
            P("dp", "tensor"),
            P("dp", "tensor"),
            P("tensor", "dp"),
        ),
        check_vma=False,
    )
```
